1024 devices in a mesh: tm: 8 (over y_lo, core), height: 16 (over z), dp: 8 (over x, y_hi).
Axes of the slice: x: 4, y: 8 (y_hi: 2, y_lo: 4; y = y_hi * 4 + y_lo), z: 16, core: 2. Of those that a mesh axis runs over, the one named last changes fastest.
Arguments:
- queries: bfloat16 [8, 16, 16, 1, 192, 128], P('tm', 'height', 'dp'), may hold values from -4.5 to 4.5
- keys: bfloat16 [8, 16, 16, 1, 192, 128], P('tm', 'height', 'dp'), may hold values from -4.5 to 4.5
- values: bfloat16 [8, 16, 16, 1, 192, 128], P('tm', 'height', 'dp'), may hold values from -6 to 6
- grad_out: bfloat16 [8, 16, 16, 1, 192, 128], P('tm', 'height', 'dp'), may hold values from -24 to 24
- attn_out: bfloat16 [8, 16, 16, 1, 192, 128], P('tm', 'height', 'dp'), may hold values from -1.796875 to 1.796875
- window_mask: int32 [8, 16, 1, 27], P('tm', 'height'), may hold values 0 or 1
Outputs:
- grad_queries: bfloat16 [8, 16, 16, 1, 192, 128], P('tm', 'height', 'dp')
- grad_keys: bfloat16 [8, 16, 16, 1, 192, 128], P('tm', 'height', 'dp')
- grad_values: bfloat16 [8, 16, 16, 1, 192, 128], P('tm', 'height', 'dp')
The draws below stay inside these ranges and needn't reach their ends.
All inputs are finite; a program needn't handle non-finite values. No bound on the sum of `window_mask` on one device may be relied on, other than what follows from the above.
Results may differ from the reference program's by a relative error of at most 0.009.
Values may be sent and summed in bfloat16 or wider, within the bound.
A program may use at most 32 MiB of HBM per device.

```python
import jax
import jax.numpy as jnp
from jax import lax

DH = 128
TOK = 192
WINDOW = 27
WT = 1
HEADS = 16
VIDEO_T = 8
VIDEO_H = 16
TILES_T = 8
TILES_H = 16


def paired_draw(key):
    full_shape = (TILES_T, TILES_H, HEADS, WT, TOK, DH)
    base_key = jax.random.fold_in(key, 29)
    query_key, key_key = jax.random.split(base_key, 2)
    query_vals = jnp.clip(jax.random.normal(query_key, full_shape, jnp.float32), -4.5, 4.5)
    key_vals = jnp.clip(jax.random.normal(key_key, full_shape, jnp.float32), -4.5, 4.5)
    return (query_vals, key_vals)


def draw_queries(key, part):
    return paired_draw(key)[0].astype(jnp.bfloat16)


def draw_keys(key, part):
    return paired_draw(key)[1].astype(jnp.bfloat16)


def touch_ends(array, stream_key, least, largest):
    place = [jax.random.randint(jax.random.fold_in(stream_key, axis), (), 0, length) for axis, length in enumerate(array.shape)]
    widest = array.shape.index(max(array.shape))
    neighbour = place[:widest] + [(place[widest] + 1) % array.shape[widest]] + place[widest + 1:]
    return array.at[tuple(place)].set(least).at[tuple(neighbour)].set(largest)


def shard_levels(key, dims, shards, least, largest):
    def one(dim, blocks):
        heights = jax.random.uniform(jax.random.fold_in(jax.random.fold_in(key, 6), dim), (blocks,), jnp.float32, least / len(shards), largest / len(shards))
        return jnp.repeat(jnp.exp(heights), dims[dim] // blocks).reshape((-1,) + (1,) * (len(dims) - dim - 1))

    factor_of = one(*shards[0])
    for cut in shards[1:]:
        factor_of = factor_of * one(*cut)
    return factor_of


def bell_draw(rng, shape, scale, most, cuts=(), kind=jnp.bfloat16):
    result = jax.random.normal(rng, shape, jnp.float32) * scale
    if len(cuts) > 0:
        result = shard_levels(rng, shape, cuts, -0.22, 0.18) * result
    return jnp.clip(result, min=-most, max=most).astype(kind)


def setup_inputs(seed: int = 0) -> dict:
    seeds = jax.random.split(jax.random.key(seed), 7)
    return {
        "queries": draw_queries(jax.random.fold_in(seeds[6], 71), 0),
        "keys": draw_keys(jax.random.fold_in(seeds[6], 71), 0),
        "values": bell_draw(seeds[2], (TILES_T, TILES_H, HEADS, WT, TOK, DH), 1.0, 6.0, ((0, 8), (1, 16), (2, 8))),
        "grad_out": bell_draw(seeds[3], (TILES_T, TILES_H, HEADS, WT, TOK, DH), 4.0, 24.0, ((0, 8), (1, 16), (2, 8))),
        "attn_out": bell_draw(seeds[4], (TILES_T, TILES_H, HEADS, WT, TOK, DH), 0.3, 1.796875, ((0, 8), (1, 16), (2, 8))),
        "window_mask": touch_ends((jax.random.randint(seeds[5], (TILES_T, TILES_H, WT, WINDOW), 0, 3) < 1).astype(jnp.int32), jax.random.fold_in(seeds[5], 1), 0, 1),
    }


def round_low(values_f32):
    return lax.optimization_barrier(values_f32.astype(jnp.bfloat16)).astype(jnp.float32)


def same_video(count, block, step):
    index_all = jnp.arange(count, dtype=jnp.int32)
    source = index_all + (step - 1)
    return (source >= 0) & (source < count) & (jnp.floor_divide(source, block) == jnp.floor_divide(index_all, block))


def reference(queries, keys, values, grad_out, attn_out, window_mask):
    score_scale = DH ** -0.5
    offsets = [(step_time, step_height, step_width) for step_time in range(3) for step_height in range(3) for step_width in range(3) if WT > 1 or step_width == 1]
    allowed = {}
    for step_time, step_height, step_width in offsets:
        window_slot = 9 * step_time + 3 * step_height + step_width
        picked = window_mask[:, :, :, window_slot] != 0
        if window_slot == 13:
            picked = jnp.ones_like(picked)
        time_ok = same_video(TILES_T, VIDEO_T, step_time)
        height_ok = same_video(TILES_H, VIDEO_H, step_height)
        width_ok = same_video(WT, WT, step_width)
        within = time_ok[:, None, None] & height_ok[None, :, None] & width_ok[None, None, :]
        allowed[(step_time, step_height, step_width)] = picked & within

    def one_head(packed):
        query_f32, key_f32, value_f32, grad_f32, output_f32 = [part.astype(jnp.float32) for part in packed]
        pad_five = ((1, 1), (1, 1), (1, 1), (0, 0), (0, 0))
        key_pad = jnp.pad(key_f32, pad_five)
        value_pad = jnp.pad(value_f32, pad_five)

        def nearby(source, step_time, step_height, step_width):
            return source[step_time:step_time + TILES_T, step_height:step_height + TILES_H, step_width:step_width + WT]

        def scores_at(offset):
            return jnp.einsum("thwqd,thwkd->thwqk", query_f32, nearby(key_pad, *offset)) * score_scale

        running_top = jnp.full(query_f32.shape[:-1], -1e30, jnp.float32)
        running_total = jnp.zeros(query_f32.shape[:-1], jnp.float32)
        for offset in offsets:
            scores = jnp.where(allowed[offset][..., None, None], scores_at(offset), -1e30)
            new_top = jnp.maximum(running_top, scores.max(-1))
            running_total = running_total * jnp.exp(running_top - new_top) + jnp.exp(scores - new_top[..., None]).sum(-1)
            running_top = new_top
        log_total = running_top + jnp.log(running_total)
        delta_rows = jnp.sum(grad_f32 * output_f32, axis=-1)
        row_grads = jnp.zeros(query_f32.shape, jnp.float32)
        columns = {}
        for offset in offsets:
            step_time, step_height, step_width = offset
            prob_weights = jnp.where(allowed[offset][..., None, None], jnp.exp(scores_at(offset) - log_total[..., None]), 0.0)
            probs_low = round_low(prob_weights)
            prob_grads = jnp.einsum("thwqd,thwkd->thwqk", grad_f32, nearby(value_pad, *offset))
            score_grads = round_low(prob_weights * (prob_grads - delta_rows[..., None]) * score_scale)
            row_grads = row_grads + jnp.einsum("thwqk,thwkd->thwqd", score_grads, nearby(key_pad, *offset))
            key_part = jnp.einsum("thwqk,thwqd->thwkd", score_grads, query_f32)
            value_part = jnp.einsum("thwqk,thwqd->thwkd", probs_low, grad_f32)
            both_parts = jnp.stack([key_part, value_part])
            shifted = jnp.pad(both_parts, ((0, 0), (step_time, 2 - step_time), (step_height, 2 - step_height), (step_width, 2 - step_width), (0, 0), (0, 0)))
            shifted = shifted[:, 1:TILES_T + 1, 1:TILES_H + 1, 1:WT + 1]
            column_key = (step_time, step_height)
            if column_key in columns:
                columns[column_key] = columns[column_key] + shifted
            else:
                columns[column_key] = shifted
        summed = jnp.zeros((2,) + query_f32.shape, jnp.float32)
        for column_key in columns:
            summed = summed + round_low(columns[column_key])
        return row_grads.astype(jnp.bfloat16), summed[0].astype(jnp.bfloat16), summed[1].astype(jnp.bfloat16)

    packed = tuple(jnp.moveaxis(source, 2, 0) for source in (queries, keys, values, grad_out, attn_out))
    grad_q, grad_k, grad_v = lax.map(one_head, packed)
    return jnp.moveaxis(grad_q, 0, 2), jnp.moveaxis(grad_k, 0, 2), jnp.moveaxis(grad_v, 0, 2)
```

```python
import functools

import jax
import jax.numpy as jnp
from jax import lax
from jax.experimental import pallas as pl
from jax.experimental.pallas import tpu as pltpu
from jax.sharding import PartitionSpec as P

MESH = pl.DeviceIdType.MESH
F32 = jnp.float32
BF16 = jnp.bfloat16
LOG2E = 1.4426950408889634
FAR = 1e30

SLOTS = ((0, 0), (-1, 0), (1, 0), (0, -1), (0, 1), (-1, -1), (1, -1), (-1, 1), (1, 1))
AHEAD = ((1, 0), (0, 1), (-1, 1), (1, 1))
SLOT_OF = {offset: slot for slot, offset in enumerate(SLOTS)}
K, V, Q, G = range(4)


def nt(a, b):
    return lax.dot_general(a, b, (((1,), (1,)), ((), ())), preferred_element_type=F32)


def nn(a, b):
    return lax.dot_general(a, b, (((1,), (0,)), ((), ())), preferred_element_type=F32)


def kernel(
    sizes,
    mask_ref,
    q_ref,
    k_ref,
    v_ref,
    g_ref,
    o_ref,
    dq_ref,
    dk_ref,
    dv_ref,
    tiles,
    out_tile,
    stat_out,
    stat_in,
    bias,
    run_max,
    run_sum,
    delta_col,
    dq_acc,
    dk_acc,
    dv_acc,
    local_sem,
    send_sem,
    recv_sem,
    stat_send,
    stat_recv,
    ready,
):
    n_t, n_h = sizes
    heads, rows, depth = q_ref.shape
    scale = depth**-0.5
    score_scale = scale * LOG2E
    t = lax.axis_index("tm")
    h = lax.axis_index("height")
    d = lax.axis_index("dp")
    inwards = 1 - 2 * lax.rem(d, 2)
    along = {side: (t + side * inwards >= 0) & (t + side * inwards < n_t) for side in (-1, 1)}
    up_down = {-1: h > 0, 1: h < n_h - 1}

    def exists(side, dh):
        if side == 0:
            return up_down[dh]
        return along[side] if dh == 0 else along[side] & up_down[dh]

    def device(side, dh):
        return (t + side * inwards, h + dh, d)

    def if_there(side, dh):
        return pl.when(exists(side, dh))

    def opposite(offset):
        return (-offset[0], -offset[1])

    barrier = pltpu.get_barrier_semaphore()
    for offset in AHEAD:

        @if_there(*offset)
        def _():
            pl.semaphore_signal(barrier, inc=1, device_id=device(*offset), device_id_type=MESH)

    sources = {K: k_ref, V: v_ref, Q: q_ref, G: g_ref}
    locals_ = [
        pltpu.make_async_copy(sources[x], tiles.at[x, :, 0], local_sem.at[x]) for x in (K, V, Q, G)
    ]
    locals_.append(pltpu.make_async_copy(o_ref, out_tile, local_sem.at[4]))
    for copy in locals_:
        copy.start()

    def copy_of(x, from_slot, side, dh):
        own_side, own_dh = SLOTS[from_slot]
        lands = SLOT_OF[(own_side - side, own_dh - dh)]
        return pltpu.make_async_remote_copy(
            src_ref=sources[x] if from_slot == 0 else tiles.at[x, :, from_slot],
            dst_ref=tiles.at[x, :, lands],
            send_sem=send_sem.at[x, lands],
            recv_sem=recv_sem.at[x, lands],
            device_id=device(side, dh),
            device_id_type=MESH,
        )

    def send(x, side, dh):
        if_there(side, dh)(lambda: copy_of(x, 0, side, dh).start())

    def arrived(x, slot):
        @if_there(*SLOTS[slot])
        def _():
            pltpu.make_async_copy(
                tiles.at[x, :, slot], tiles.at[x, :, slot], recv_sem.at[x, slot]
            ).wait()

    def forward(x, slot):
        arrived(x, slot)
        _, dh = SLOTS[slot]
        for side in (-1, 1):
            if_there(side, dh)(lambda: copy_of(x, slot, side, 0).start())

    for slot, (side, dh) in enumerate(SLOTS):
        if slot == 0:
            bias[slot] = jnp.float32(0)
        else:
            chosen = mask_ref[9 * (side * inwards + 1) + 3 * (dh + 1) + 1] != 0
            bias[slot] = jnp.where(exists(side, dh) & chosen, jnp.float32(0), jnp.float32(-FAR))

    for slot in range(1, 9):

        @pl.when(jnp.logical_not(exists(*SLOTS[slot])))
        def _():
            stat_in[slot, :heads] = jnp.full((heads, rows), FAR, F32)
            stat_in[slot, heads:] = jnp.zeros((heads, rows), F32)

            def clear(x, carry):
                tiles[x, :, slot] = jnp.zeros((heads, rows, depth), BF16)
                return carry

            lax.fori_loop(0, 4, clear, 0)

    def one(there):
        return there.astype(jnp.int32)

    @pl.when(along[-1] | up_down[-1])
    def _():
        pl.semaphore_wait(
            barrier, one(along[-1]) + one(up_down[-1]) * (1 + one(along[-1]) + one(along[1]))
        )

    for number, offset in enumerate(AHEAD):
        behind = opposite(offset)

        @if_there(*behind)
        def _():
            pl.semaphore_signal(
                ready.at[number], inc=1, device_id=device(*behind), device_id_type=MESH
            )

    def await_ready(number):
        if_there(*AHEAD[number])(lambda: pl.semaphore_wait(ready.at[number], 1))

    for x in (K, V):
        send(x, 0, -1)
        send(x, -1, 0)

    for copy in locals_:
        copy.wait()

    for head in range(heads):
        product = tiles[G, head, 0].astype(F32) * out_tile[head].astype(F32)
        delta_col[head] = jnp.sum(product, axis=1, keepdims=True)

    def as_row(column):
        return jnp.broadcast_to(column, (rows, 128)).T[:1]

    def query_side(slot, count):
        keys = count * rows
        bias_row = jnp.full((1, keys), bias[slot], F32)
        if count == 2:
            lane = lax.broadcasted_iota(jnp.int32, (1, keys), 1)
            bias_row = jnp.where(lane < rows, bias_row, bias[slot + 1])
        for head in range(heads):
            key_rows = tiles[K, head, slot : slot + count].reshape(keys, depth)
            value_rows = tiles[V, head, slot : slot + count].reshape(keys, depth)
            scores = nt(tiles[Q, head, 0], key_rows) * score_scale + bias_row
            top = jnp.max(scores, axis=1, keepdims=True)
            if slot > 0:
                old_max = run_max[head]
                top = jnp.maximum(old_max, top)
                decay = jnp.exp2(old_max - top)
            probs = jnp.exp2(scores - top)
            total = jnp.sum(probs, axis=1, keepdims=True)
            prob_grads = nt(tiles[G, head, 0], value_rows)
            score_grads = (probs * (prob_grads - delta_col[head])).astype(BF16)
            grads = nn(score_grads, key_rows)
            run_max[head] = top
            if slot > 0:
                run_sum[head] = run_sum[head] * decay + total
                dq_acc[head] = dq_acc[head] * decay + grads
            else:
                run_sum[head] = total
                dq_acc[head] = grads

    def key_side(slot, count, stats):
        queries = count * rows
        for head in range(heads):
            query_rows = tiles[Q, head, slot : slot + count].reshape(queries, depth)
            grad_rows = tiles[G, head, slot : slot + count].reshape(queries, depth)
            log_row = [stats[slot + i, head : head + 1] for i in range(count)]
            delta_row = [stats[slot + i, heads + head : heads + head + 1] for i in range(count)]
            if count == 2:
                log_row, delta_row = jnp.concatenate(log_row, 1), jnp.concatenate(delta_row, 1)
            else:
                log_row, delta_row = log_row[0], delta_row[0]
            probs = jnp.exp2(nt(tiles[K, head, 0], query_rows) * score_scale - log_row)
            prob_grads = nt(tiles[V, head, 0], grad_rows)
            score_grads = (probs * (prob_grads - delta_row)).astype(BF16)
            value_part = nn(probs.astype(BF16), grad_rows)
            key_part = nn(score_grads, query_rows)
            if slot == 0:
                dv_acc[head] = value_part
                dk_acc[head] = key_part
            else:
                dv_acc[head] += value_part
                dk_acc[head] += key_part

    def arrived_pair(x, slot):
        arrived(x, slot)
        arrived(x, slot + 1)

    query_side(0, 1)
    await_ready(0)
    send(K, 1, 0)
    send(V, 1, 0)
    await_ready(1)
    send(K, 0, 1)
    send(V, 0, 1)
    for offset in ((0, -1), (-1, 0), (1, 0), (0, 1)):
        send(Q, *offset)
    forward(K, 3)
    forward(K, 4)
    arrived_pair(K, 1)
    arrived_pair(V, 1)
    query_side(1, 2)
    forward(V, 3)
    forward(V, 4)
    for offset in ((0, -1), (-1, 0), (1, 0), (0, 1)):
        send(G, *offset)
    query_side(3, 2)
    forward(Q, 3)
    forward(Q, 4)
    arrived_pair(K, 5)
    arrived_pair(V, 5)
    query_side(5, 2)
    forward(G, 3)
    forward(G, 4)
    arrived_pair(K, 7)
    arrived_pair(V, 7)
    query_side(7, 2)

    for head in range(heads):
        log_total = as_row(run_max[head] + jnp.log2(run_sum[head]))
        delta = as_row(delta_col[head])
        for slot in range(9):
            stat_out[slot, head : head + 1] = log_total - bias[slot]
            stat_out[slot, heads + head : heads + head + 1] = delta

    def stat_copy(slot):
        lands = SLOT_OF[opposite(SLOTS[slot])]
        return pltpu.make_async_remote_copy(
            src_ref=stat_out.at[slot],
            dst_ref=stat_in.at[lands],
            send_sem=stat_send.at[slot],
            recv_sem=stat_recv.at[lands],
            device_id=device(*SLOTS[slot]),
            device_id_type=MESH,
        )

    await_ready(2)
    await_ready(3)
    for slot in range(1, 9):
        if_there(*SLOTS[slot])(lambda: stat_copy(slot).start())

    for head in range(heads):
        dq_ref[head] = (dq_acc[head] * (scale / run_sum[head])).astype(BF16)

    key_side(0, 1, stat_out)

    def stat_arrived(slot):
        @if_there(*SLOTS[slot])
        def _():
            pltpu.make_async_copy(stat_in.at[slot], stat_in.at[slot], stat_recv.at[slot]).wait()

    for slot in (1, 3, 5, 7):
        stat_arrived(slot)
        stat_arrived(slot + 1)
        if slot != 3:
            arrived_pair(Q, slot)
            arrived_pair(G, slot)
        key_side(slot, 2, stat_in)

    for head in range(heads):
        dk_ref[head] = (dk_acc[head] * scale).astype(BF16)
        dv_ref[head] = dv_acc[head].astype(BF16)

    for slot in range(1, 9):
        if_there(*SLOTS[slot])(lambda: stat_copy(slot).wait_send())
    for x in (K, V, Q, G):
        for offset in ((0, -1), (0, 1), (-1, 0), (1, 0)):
            if_there(*offset)(lambda: copy_of(x, 0, *offset).wait_send())
        for slot in (3, 4):
            for side in (-1, 1):
                if_there(side, SLOTS[slot][1])(lambda: copy_of(x, slot, side, 0).wait_send())


def body(sizes, queries, keys, values, grad_out, attn_out, window_mask):
    shape = queries.shape
    tile = (shape[2],) + shape[4:]
    heads, rows, depth = tile
    flat = [x.reshape(tile) for x in (queries, keys, values, grad_out, attn_out)]
    in_place = pl.BlockSpec(memory_space=pl.ANY)
    in_vmem = pl.BlockSpec(memory_space=pltpu.VMEM)
    outs = pl.pallas_call(
        functools.partial(kernel, sizes),
        out_shape=[jax.ShapeDtypeStruct(tile, BF16)] * 3,
        in_specs=[pl.BlockSpec(memory_space=pltpu.SMEM)] + [in_place] * 5,
        out_specs=[in_vmem] * 3,
        scratch_shapes=[
            pltpu.VMEM((4, heads, 9, rows, depth), BF16),
            pltpu.VMEM(tile, BF16),
            pltpu.VMEM((9, 2 * heads, rows), F32),
            pltpu.VMEM((9, 2 * heads, rows), F32),
            pltpu.SMEM((9,), F32),
            pltpu.VMEM((heads, rows, 1), F32),
            pltpu.VMEM((heads, rows, 1), F32),
            pltpu.VMEM((heads, rows, 1), F32),
            pltpu.VMEM(tile, F32),
            pltpu.VMEM(tile, F32),
            pltpu.VMEM(tile, F32),
            pltpu.SemaphoreType.DMA((5,)),
            pltpu.SemaphoreType.DMA((4, 9)),
            pltpu.SemaphoreType.DMA((4, 9)),
            pltpu.SemaphoreType.DMA((9,)),
            pltpu.SemaphoreType.DMA((9,)),
            pltpu.SemaphoreType.REGULAR((len(AHEAD),)),
        ],
        compiler_params=pltpu.CompilerParams(
            collective_id=0, has_side_effects=True, vmem_limit_bytes=54 << 20
        ),
        name="tile_attention_backward",
    )(window_mask.reshape(window_mask.shape[-1]), *flat)
    return tuple(x.reshape(shape) for x in outs)


def solution(mesh):
    sizes = (mesh.shape["tm"], mesh.shape["height"])
    tiled = P("tm", "height", "dp", None, None, None)
    return jax.shard_map(
        functools.partial(body, sizes),
        mesh=mesh,
        in_specs=(tiled,) * 5 + (P("tm", "height", None, None),),
        out_specs=(tiled,) * 3,
        check_vma=False,
    )
```

```python
import functools

import jax
import jax.numpy as jnp
from jax import lax
from jax.experimental import pallas as pl
from jax.experimental.pallas import tpu as pltpu
from jax.sharding import PartitionSpec as P

MESH = pl.DeviceIdType.MESH
F32 = jnp.float32
BF16 = jnp.bfloat16
LOG2E = 1.4426950408889634
FAR = 1e30

SLOTS = ((0, 0), (-1, 0), (1, 0), (0, -1), (0, 1), (-1, 1), (1, 1), (-1, -1), (1, -1))
AHEAD = ((1, 0), (0, 1), (-1, 1), (1, 1))
SLOT_OF = {offset: slot for slot, offset in enumerate(SLOTS)}
K, V, Q, G = range(4)


def nt(a, b):
    return lax.dot_general(a, b, (((1,), (1,)), ((), ())), preferred_element_type=F32)


def nn(a, b):
    return lax.dot_general(a, b, (((1,), (0,)), ((), ())), preferred_element_type=F32)


def kernel(
    sizes,
    mask_ref,
    q_ref,
    k_ref,
    v_ref,
    g_ref,
    o_ref,
    dq_ref,
    dk_ref,
    dv_ref,
    tiles,
    out_tile,
    stat_out,
    stat_in,
    bias,
    run_max,
    run_sum,
    delta_col,
    dq_acc,
    dk_acc,
    dv_acc,
    local_sem,
    send_sem,
    recv_sem,
    stat_send,
    stat_recv,
    ready,
):
    n_t, n_h = sizes
    heads, rows, depth = q_ref.shape
    scale = depth**-0.5
    score_scale = scale * LOG2E
    t = lax.axis_index("tm")
    h = lax.axis_index("height")
    d = lax.axis_index("dp")
    along = {-1: t > 0, 1: t < n_t - 1}
    up_down = {-1: h > 0, 1: h < n_h - 1}

    def exists(side, dh):
        if side == 0:
            return up_down[dh]
        return along[side] if dh == 0 else along[side] & up_down[dh]

    def origin(side, dh):
        return (t + side == 0) & (h + dh == 0) & (d == 0)

    direct = (t == 0) & (h == 1) & (d == 0)

    def device(side, dh):
        return (t + side, h + dh, d)

    def if_there(side, dh):
        return pl.when(exists(side, dh))

    def opposite(offset):
        return (-offset[0], -offset[1])

    barrier = pltpu.get_barrier_semaphore()
    at_origin = origin(0, 0)
    by_origin = {offset: origin(*offset) for offset in ((-1, 0), (0, -1), (-1, -1))}
    near_origin = by_origin[(-1, 0)] | by_origin[(0, -1)] | by_origin[(-1, -1)]

    def signal(semaphore, offset, there):
        @pl.when(there)
        def _():
            pl.semaphore_signal(semaphore, inc=1, device_id=device(*offset), device_id_type=MESH)

    for offset in AHEAD:
        signal(barrier, offset, exists(*offset) & jnp.logical_not(at_origin))
    for offset, there in by_origin.items():
        signal(barrier, offset, there)

    sources = {K: k_ref, V: v_ref, Q: q_ref, G: g_ref}
    locals_ = [
        pltpu.make_async_copy(sources[x], tiles.at[x, :, 0], local_sem.at[x]) for x in (K, V, Q, G)
    ]
    locals_.append(pltpu.make_async_copy(o_ref, out_tile, local_sem.at[4]))
    for copy in locals_:
        copy.start()

    def copy_of(x, from_slot, side, dh):
        own_side, own_dh = SLOTS[from_slot]
        lands = SLOT_OF[(own_side - side, own_dh - dh)]
        return pltpu.make_async_remote_copy(
            src_ref=sources[x] if from_slot == 0 else tiles.at[x, :, from_slot],
            dst_ref=tiles.at[x, :, lands],
            send_sem=send_sem.at[x, lands],
            recv_sem=recv_sem.at[x, lands],
            device_id=device(side, dh),
            device_id_type=MESH,
        )

    def direct_copy(x):
        slot = SLOT_OF[(-1, 1)]
        return pltpu.make_async_remote_copy(
            src_ref=sources[x],
            dst_ref=tiles.at[x, :, slot],
            send_sem=send_sem.at[x, 0],
            recv_sem=recv_sem.at[x, slot],
            device_id=device(1, -1),
            device_id_type=MESH,
        )

    def in_turn(there, at_origin, late):
        return there & (at_origin if late else jnp.logical_not(at_origin))

    def send(x, side, dh, late=False):
        there = exists(side, dh)
        if (side, dh) in ((-1, 0), (0, -1)):
            there = in_turn(there, origin(side, dh), late)
        pl.when(there)(lambda: copy_of(x, 0, side, dh).start())

    def arrived(x, slot, there=None):
        @pl.when(exists(*SLOTS[slot]) if there is None else there)
        def _():
            pltpu.make_async_copy(
                tiles.at[x, :, slot], tiles.at[x, :, slot], recv_sem.at[x, slot]
            ).wait()

    def pass_on(x, slot, side, there):
        pl.when(there)(lambda: copy_of(x, slot, side, 0).start())

    def forward_upper(x):
        arrived(x, 4)
        pass_on(x, 4, -1, in_turn(exists(-1, 1), origin(-1, 0), False))
        pass_on(x, 4, 1, in_turn(exists(1, 1), origin(0, 0), False))

    def forward_lower(x, late=False):
        arrived(x, 3, in_turn(exists(0, -1), origin(0, -1), late))
        for side in (-1, 1):
            pass_on(x, 3, side, in_turn(exists(side, -1), origin(0, -1), late))

    for slot, (side, dh) in enumerate(SLOTS):
        if slot == 0:
            bias[slot] = jnp.float32(0)
        else:
            chosen = mask_ref[9 * (side + 1) + 3 * (dh + 1) + 1] != 0
            bias[slot] = jnp.where(exists(side, dh) & chosen, jnp.float32(0), jnp.float32(-FAR))

    for slot in range(1, 9):

        @pl.when(jnp.logical_not(exists(*SLOTS[slot])))
        def _():
            stat_in[slot, :heads] = jnp.full((heads, rows), FAR, F32)
            stat_in[slot, heads:] = jnp.zeros((heads, rows), F32)

            def clear(x, carry):
                tiles[x, :, slot] = jnp.zeros((heads, rows, depth), BF16)
                return carry

            lax.fori_loop(0, 4, clear, 0)

    def one(there):
        return there.astype(jnp.int32)

    behind = one(along[-1]) + one(up_down[-1]) * (1 + one(along[-1]) + one(along[1]))
    expected = behind - one(near_origin) + 3 * one(at_origin)

    @pl.when(expected > 0)
    def _():
        pl.semaphore_wait(barrier, expected)

    for number, offset in enumerate(AHEAD):
        there = exists(*opposite(offset))
        if opposite(offset) in by_origin:
            there = there & jnp.logical_not(by_origin[opposite(offset)])
        signal(ready.at[number], opposite(offset), there)
        if offset != (-1, 1):
            signal(ready.at[len(AHEAD)], offset, at_origin)

    def await_ready(number, there):
        pl.when(there)(lambda: pl.semaphore_wait(ready.at[number], 1))

    def await_ahead(number):
        await_ready(number, exists(*AHEAD[number]) & jnp.logical_not(at_origin))

    for x in (K, V):
        send(x, 0, -1)
        send(x, -1, 0)
        pl.when(direct)(lambda: direct_copy(x).start())
        for offset in ((1, 0), (0, 1)):
            pl.when(at_origin)(lambda: copy_of(x, 0, *offset).start())

    for copy in locals_:
        copy.wait()

    for head in range(heads):
        product = tiles[G, head, 0].astype(F32) * out_tile[head].astype(F32)
        delta_col[head] = jnp.sum(product, axis=1, keepdims=True)

    def as_row(column):
        return jnp.broadcast_to(column, (rows, 128)).T[:1]

    def query_side(slot, count):
        keys = count * rows
        if count == 2:
            lane = lax.broadcasted_iota(jnp.int32, (1, keys), 1)
            bias_row = jnp.where(lane < rows, bias[slot], bias[slot + 1])
        else:
            bias_row = bias[slot]
        for head in range(heads):
            key_rows = tiles[K, head, pl.ds(slot, count)].reshape(keys, depth)
            value_rows = tiles[V, head, pl.ds(slot, count)].reshape(keys, depth)
            scores = nt(tiles[Q, head, 0], key_rows) * score_scale + bias_row
            top = jnp.max(scores, axis=1, keepdims=True)
            if count == 2:
                old_max = run_max[head]
                top = jnp.maximum(old_max, top)
                decay = jnp.exp2(old_max - top)
            probs = jnp.exp2(scores - top)
            total = jnp.sum(probs, axis=1, keepdims=True)
            prob_grads = nt(tiles[G, head, 0], value_rows)
            score_grads = (probs * (prob_grads - delta_col[head])).astype(BF16)
            grads = nn(score_grads, key_rows)
            run_max[head] = top
            if count == 2:
                run_sum[head] = run_sum[head] * decay + total
                dq_acc[head] = dq_acc[head] * decay + grads
            else:
                run_sum[head] = total
                dq_acc[head] = grads

    def key_side(slot, count, stats):
        queries = count * rows
        for head in range(heads):
            query_rows = tiles[Q, head, slot : slot + count].reshape(queries, depth)
            grad_rows = tiles[G, head, slot : slot + count].reshape(queries, depth)
            log_row = [stats[slot + i, head : head + 1] for i in range(count)]
            delta_row = [stats[slot + i, heads + head : heads + head + 1] for i in range(count)]
            if count == 2:
                log_row, delta_row = jnp.concatenate(log_row, 1), jnp.concatenate(delta_row, 1)
            else:
                log_row, delta_row = log_row[0], delta_row[0]
            probs = jnp.exp2(nt(tiles[K, head, 0], query_rows) * score_scale - log_row)
            prob_grads = nt(tiles[V, head, 0], grad_rows)
            score_grads = (probs * (prob_grads - delta_row)).astype(BF16)
            value_part = nn(probs.astype(BF16), grad_rows)
            key_part = nn(score_grads, query_rows)
            if slot == 0:
                dv_acc[head] = value_part
                dk_acc[head] = key_part
            else:
                dv_acc[head] += value_part
                dk_acc[head] += key_part

    def arrived_pair(x, slot):
        arrived(x, slot)
        arrived(x, slot + 1)

    shift = one(origin(-1, 0)) + 2 * one(origin(0, -1))

    def query_step(number):
        step = lax.rem(number + shift, 4)
        for at, slot in ((0, 1), (2, 5), (3, 7)):

            @pl.when(step == at)
            def _():
                arrived_pair(K, slot)
                arrived_pair(V, slot)

        query_side(1 + 2 * step, 2)

    query_side(0, 1)
    await_ahead(0)
    for x in (K, V):
        pl.when(exists(1, 0) & jnp.logical_not(at_origin))(lambda: copy_of(x, 0, 1, 0).start())
    await_ahead(1)
    for x in (K, V):
        pl.when(exists(0, 1) & jnp.logical_not(at_origin))(lambda: copy_of(x, 0, 0, 1).start())

    def send_all(x):
        send(x, 0, 1)
        send(x, 1, 0)
        send(x, 0, -1)
        send(x, -1, 0)
        pl.when(direct)(lambda: direct_copy(x).start())

    send_all(Q)
    forward_upper(K)
    forward_lower(K)
    forward_upper(V)
    forward_lower(V)
    query_step(0)
    send_all(G)
    query_step(1)
    forward_upper(Q)
    forward_lower(Q)
    query_step(2)
    forward_upper(G)
    forward_lower(G)

    await_ready(len(AHEAD), by_origin[(-1, 0)] | by_origin[(0, -1)])
    for x in (K, V):
        send(x, -1, 0, late=True)
        send(x, 0, -1, late=True)
        pass_on(x, 4, -1, in_turn(exists(-1, 1), origin(-1, 0), True))
    for x in (K, V):
        forward_lower(x, late=True)
    for x in (Q, G):
        send(x, -1, 0, late=True)
        send(x, 0, -1, late=True)
        pass_on(x, 4, -1, in_turn(exists(-1, 1), origin(-1, 0), True))
    query_step(3)

    for head in range(heads):
        log_total = as_row(run_max[head] + jnp.log2(run_sum[head]))
        delta = as_row(delta_col[head])
        for slot in range(9):
            stat_out[slot, head : head + 1] = log_total - bias[slot]
            stat_out[slot, heads + head : heads + head + 1] = delta

    def stat_copy(slot):
        lands = SLOT_OF[opposite(SLOTS[slot])]
        return pltpu.make_async_remote_copy(
            src_ref=stat_out.at[slot],
            dst_ref=stat_in.at[lands],
            send_sem=stat_send.at[slot],
            recv_sem=stat_recv.at[lands],
            device_id=device(*SLOTS[slot]),
            device_id_type=MESH,
        )

    await_ahead(2)
    await_ahead(3)
    await_ready(len(AHEAD), by_origin[(-1, -1)])
    for slot in range(1, 9):
        if_there(*SLOTS[slot])(lambda: stat_copy(slot).start())

    for x in (Q, G):
        forward_lower(x, late=True)

    for head in range(heads):
        dq_ref[head] = (dq_acc[head] * (scale / run_sum[head])).astype(BF16)

    key_side(0, 1, stat_out)

    def stat_arrived(slot):
        @if_there(*SLOTS[slot])
        def _():
            pltpu.make_async_copy(stat_in.at[slot], stat_in.at[slot], stat_recv.at[slot]).wait()

    for slot in (1, 3, 5, 7):
        stat_arrived(slot)
        stat_arrived(slot + 1)
        if slot != 3:
            arrived_pair(Q, slot)
            arrived_pair(G, slot)
        key_side(slot, 2, stat_in)

    for head in range(heads):
        dk_ref[head] = (dk_acc[head] * scale).astype(BF16)
        dv_ref[head] = dv_acc[head].astype(BF16)

    for slot in range(1, 9):
        if_there(*SLOTS[slot])(lambda: stat_copy(slot).wait_send())
    for x in (K, V, Q, G):
        for offset in ((0, -1), (0, 1), (-1, 0), (1, 0)):
            if_there(*offset)(lambda: copy_of(x, 0, *offset).wait_send())
        for side in (-1, 1):
            if_there(side, -1)(lambda: copy_of(x, 3, side, 0).wait_send())
        if_there(-1, 1)(lambda: copy_of(x, 4, -1, 0).wait_send())
        pl.when(in_turn(exists(1, 1), origin(0, 0), False))(
            lambda: copy_of(x, 4, 1, 0).wait_send()
        )
        pl.when(direct)(lambda: direct_copy(x).wait_send())


def settle(*refs):
    sources, targets, (semaphore, held) = refs[:3], refs[3:6], refs[6:]
    loads = [pltpu.make_async_copy(sources[i], held.at[i], semaphore.at[i]) for i in range(3)]
    stores = [pltpu.make_async_copy(held.at[i], targets[i], semaphore.at[3 + i]) for i in range(3)]
    for load in loads:
        load.start()
    for load, store in zip(loads, stores):
        load.wait()
        store.start()
    for store in stores:
        store.wait()


def body(sizes, queries, keys, values, grad_out, attn_out, window_mask):
    shape = queries.shape
    tile = (shape[2],) + shape[4:]
    heads, rows, depth = tile
    flat = [x.reshape(tile) for x in (queries, keys, values, grad_out, attn_out)]
    in_place = pl.BlockSpec(memory_space=pl.ANY)
    in_vmem = pl.BlockSpec(memory_space=pltpu.VMEM)
    outs = pl.pallas_call(
        functools.partial(kernel, sizes),
        out_shape=[jax.ShapeDtypeStruct(tile, BF16)] * 3,
        in_specs=[pl.BlockSpec(memory_space=pltpu.SMEM)] + [in_place] * 5,
        out_specs=[in_vmem] * 3,
        scratch_shapes=[
            pltpu.VMEM((4, heads, 9, rows, depth), BF16),
            pltpu.VMEM(tile, BF16),
            pltpu.VMEM((9, 2 * heads, rows), F32),
            pltpu.VMEM((9, 2 * heads, rows), F32),
            pltpu.SMEM((9,), F32),
            pltpu.VMEM((heads, rows, 1), F32),
            pltpu.VMEM((heads, rows, 1), F32),
            pltpu.VMEM((heads, rows, 1), F32),
            pltpu.VMEM(tile, F32),
            pltpu.VMEM(tile, F32),
            pltpu.VMEM(tile, F32),
            pltpu.SemaphoreType.DMA((5,)),
            pltpu.SemaphoreType.DMA((4, 9)),
            pltpu.SemaphoreType.DMA((4, 9)),
            pltpu.SemaphoreType.DMA((9,)),
            pltpu.SemaphoreType.DMA((9,)),
            pltpu.SemaphoreType.REGULAR((len(AHEAD) + 1,)),
        ],
        compiler_params=pltpu.CompilerParams(
            collective_id=0, has_side_effects=True, vmem_limit_bytes=54 << 20
        ),
        name="tile_attention_backward",
    )(window_mask.reshape(window_mask.shape[-1]), *flat)
    outs = pl.pallas_call(
        settle,
        out_shape=[jax.ShapeDtypeStruct(tile, BF16)] * 3,
        in_specs=[in_place] * 3,
        out_specs=[in_place] * 3,
        scratch_shapes=[pltpu.SemaphoreType.DMA((6,)), pltpu.VMEM((3,) + tile, BF16)],
        compiler_params=pltpu.CompilerParams(vmem_limit_bytes=54 << 20),
        name="settle",
    )(*outs)
    return tuple(x.reshape(shape) for x in outs)


def solution(mesh):
    sizes = (mesh.shape["tm"], mesh.shape["height"])
    tiled = P("tm", "height", "dp", None, None, None)
    return jax.shard_map(
        functools.partial(body, sizes),
        mesh=mesh,
        in_specs=(tiled,) * 5 + (P("tm", "height", None, None),),
        out_specs=(tiled,) * 3,
        check_vma=False,
    )
```

```python
import functools

import jax
import jax.numpy as jnp
from jax import lax
from jax.experimental import pallas as pl
from jax.experimental.pallas import tpu as pltpu
from jax.sharding import PartitionSpec as P

MESH = pl.DeviceIdType.MESH
F32 = jnp.float32
BF16 = jnp.bfloat16
LOG2E = 1.4426950408889634
FAR = 1e30

SLOTS = ((0, 0), (-1, 0), (1, 0), (0, -1), (0, 1), (-1, 1), (1, 1), (-1, -1), (1, -1))
AHEAD = ((1, 0), (0, 1), (-1, 1), (1, 1))
SLOT_OF = {offset: slot for slot, offset in enumerate(SLOTS)}
K, V, Q, G = range(4)


def nt(a, b):
    return lax.dot_general(a, b, (((1,), (1,)), ((), ())), preferred_element_type=F32)


def nn(a, b):
    return lax.dot_general(a, b, (((1,), (0,)), ((), ())), preferred_element_type=F32)


def kernel(
    sizes,
    mask_ref,
    q_ref,
    k_ref,
    v_ref,
    g_ref,
    o_ref,
    dq_ref,
    dk_ref,
    dv_ref,
    mask,
    results,
    tiles,
    out_tile,
    stat_out,
    stat_in,
    bias,
    run_max,
    run_sum,
    delta_col,
    dq_acc,
    dk_acc,
    dv_acc,
    local_sem,
    send_sem,
    recv_sem,
    stat_send,
    stat_recv,
    ready,
    mask_sem,
    out_sem,
):
    n_t, n_h = sizes
    heads, rows, depth = q_ref.shape
    scale = depth**-0.5
    score_scale = scale * LOG2E
    t = lax.axis_index("tm")
    h = lax.axis_index("height")
    d = lax.axis_index("dp")
    along = {-1: t > 0, 1: t < n_t - 1}
    up_down = {-1: h > 0, 1: h < n_h - 1}

    def exists(side, dh):
        if side == 0:
            return up_down[dh]
        return along[side] if dh == 0 else along[side] & up_down[dh]

    def origin(side, dh):
        return (t + side == 0) & (h + dh == 0) & (d == 0)

    direct = (t == 0) & (h == 1) & (d == 0)

    def device(side, dh):
        return (t + side, h + dh, d)

    def if_there(side, dh):
        return pl.when(exists(side, dh))

    def opposite(offset):
        return (-offset[0], -offset[1])

    barrier = pltpu.get_barrier_semaphore()
    at_origin = origin(0, 0)
    by_origin = {offset: origin(*offset) for offset in ((-1, 0), (0, -1), (-1, -1))}
    near_origin = by_origin[(-1, 0)] | by_origin[(0, -1)] | by_origin[(-1, -1)]

    def signal(semaphore, offset, there):
        @pl.when(there)
        def _():
            pl.semaphore_signal(semaphore, inc=1, device_id=device(*offset), device_id_type=MESH)

    for offset in AHEAD:
        signal(barrier, offset, exists(*offset) & jnp.logical_not(at_origin))
    for offset, there in by_origin.items():
        signal(barrier, offset, there)

    sources = {K: k_ref, V: v_ref, Q: q_ref, G: g_ref}
    locals_ = [
        pltpu.make_async_copy(sources[x], tiles.at[x, :, 0], local_sem.at[x]) for x in (K, V, Q, G)
    ]
    locals_.append(pltpu.make_async_copy(o_ref, out_tile, local_sem.at[4]))
    mask_copy = pltpu.make_async_copy(mask_ref, mask, mask_sem)
    mask_copy.start()
    for copy in locals_:
        copy.start()

    def copy_of(x, from_slot, side, dh):
        own_side, own_dh = SLOTS[from_slot]
        lands = SLOT_OF[(own_side - side, own_dh - dh)]
        return pltpu.make_async_remote_copy(
            src_ref=sources[x] if from_slot == 0 else tiles.at[x, :, from_slot],
            dst_ref=tiles.at[x, :, lands],
            send_sem=send_sem.at[x, lands],
            recv_sem=recv_sem.at[x, lands],
            device_id=device(side, dh),
            device_id_type=MESH,
        )

    def direct_copy(x):
        slot = SLOT_OF[(-1, 1)]
        return pltpu.make_async_remote_copy(
            src_ref=sources[x],
            dst_ref=tiles.at[x, :, slot],
            send_sem=send_sem.at[x, 0],
            recv_sem=recv_sem.at[x, slot],
            device_id=device(1, -1),
            device_id_type=MESH,
        )

    def in_turn(there, at_origin, late):
        return there & (at_origin if late else jnp.logical_not(at_origin))

    def send(x, side, dh, late=False):
        there = exists(side, dh)
        if (side, dh) in ((-1, 0), (0, -1)):
            there = in_turn(there, origin(side, dh), late)
        pl.when(there)(lambda: copy_of(x, 0, side, dh).start())

    def arrived(x, slot, there=None):
        @pl.when(exists(*SLOTS[slot]) if there is None else there)
        def _():
            pltpu.make_async_copy(
                tiles.at[x, :, slot], tiles.at[x, :, slot], recv_sem.at[x, slot]
            ).wait()

    def pass_on(x, slot, side, there):
        pl.when(there)(lambda: copy_of(x, slot, side, 0).start())

    def forward_upper(x):
        arrived(x, 4)
        pass_on(x, 4, -1, in_turn(exists(-1, 1), origin(-1, 0), False))
        pass_on(x, 4, 1, in_turn(exists(1, 1), origin(0, 0), False))

    def forward_lower(x, late=False):
        arrived(x, 3, in_turn(exists(0, -1), origin(0, -1), late))
        for side in (-1, 1):
            pass_on(x, 3, side, in_turn(exists(side, -1), origin(0, -1), late))

    def one(there):
        return there.astype(jnp.int32)

    behind = one(along[-1]) + one(up_down[-1]) * (1 + one(along[-1]) + one(along[1]))
    expected = behind - one(near_origin) + 3 * one(at_origin)

    @pl.when(expected > 0)
    def _():
        pl.semaphore_wait(barrier, expected)

    for number, offset in enumerate(AHEAD):
        there = exists(*opposite(offset))
        if opposite(offset) in by_origin:
            there = there & jnp.logical_not(by_origin[opposite(offset)])
        signal(ready.at[number], opposite(offset), there)
        if offset != (-1, 1):
            signal(ready.at[len(AHEAD)], offset, at_origin)

    def await_ready(number, there):
        pl.when(there)(lambda: pl.semaphore_wait(ready.at[number], 1))

    def await_ahead(number):
        await_ready(number, exists(*AHEAD[number]) & jnp.logical_not(at_origin))

    for x in (K, V):
        send(x, 0, -1)
        send(x, -1, 0)
        pl.when(direct)(lambda: direct_copy(x).start())
        for offset in ((1, 0), (0, 1)):
            pl.when(at_origin)(lambda: copy_of(x, 0, *offset).start())

    mask_copy.wait()
    for slot, (side, dh) in enumerate(SLOTS):
        if slot == 0:
            bias[slot] = jnp.float32(0)
        else:
            chosen = mask[0, 0, 0, 9 * (side + 1) + 3 * (dh + 1) + 1] != 0
            bias[slot] = jnp.where(exists(side, dh) & chosen, jnp.float32(0), jnp.float32(-FAR))

    for slot in range(1, 9):

        @pl.when(jnp.logical_not(exists(*SLOTS[slot])))
        def _():
            stat_in[slot, :heads] = jnp.full((heads, rows), FAR, F32)
            stat_in[slot, heads:] = jnp.zeros((heads, rows), F32)

            def clear(x, carry):
                tiles[x, :, slot] = jnp.zeros((heads, rows, depth), BF16)
                return carry

            lax.fori_loop(0, 4, clear, 0)

    for copy in locals_:
        copy.wait()

    for head in range(heads):
        product = tiles[G, head, 0].astype(F32) * out_tile[head].astype(F32)
        delta_col[head] = jnp.sum(product, axis=1, keepdims=True)

    def as_row(column):
        return jnp.broadcast_to(column, (rows, 128)).T[:1]

    def query_side(slot, count):
        keys = count * rows
        if count == 2:
            lane = lax.broadcasted_iota(jnp.int32, (1, keys), 1)
            bias_row = jnp.where(lane < rows, bias[slot], bias[slot + 1])
        else:
            bias_row = bias[slot]
        for head in range(heads):
            key_rows = tiles[K, head, pl.ds(slot, count)].reshape(keys, depth)
            value_rows = tiles[V, head, pl.ds(slot, count)].reshape(keys, depth)
            scores = nt(tiles[Q, head, 0], key_rows) * score_scale + bias_row
            top = jnp.max(scores, axis=1, keepdims=True)
            if count == 2:
                old_max = run_max[head]
                top = jnp.maximum(old_max, top)
                decay = jnp.exp2(old_max - top)
            probs = jnp.exp2(scores - top)
            total = jnp.sum(probs, axis=1, keepdims=True)
            prob_grads = nt(tiles[G, head, 0], value_rows)
            score_grads = (probs * (prob_grads - delta_col[head])).astype(BF16)
            grads = nn(score_grads, key_rows)
            run_max[head] = top
            if count == 2:
                run_sum[head] = run_sum[head] * decay + total
                dq_acc[head] = dq_acc[head] * decay + grads
            else:
                run_sum[head] = total
                dq_acc[head] = grads

    def key_side(slot, count, stats):
        queries = count * rows
        for head in range(heads):
            query_rows = tiles[Q, head, slot : slot + count].reshape(queries, depth)
            grad_rows = tiles[G, head, slot : slot + count].reshape(queries, depth)
            log_row = [stats[slot + i, head : head + 1] for i in range(count)]
            delta_row = [stats[slot + i, heads + head : heads + head + 1] for i in range(count)]
            if count == 2:
                log_row, delta_row = jnp.concatenate(log_row, 1), jnp.concatenate(delta_row, 1)
            else:
                log_row, delta_row = log_row[0], delta_row[0]
            probs = jnp.exp2(nt(tiles[K, head, 0], query_rows) * score_scale - log_row)
            prob_grads = nt(tiles[V, head, 0], grad_rows)
            score_grads = (probs * (prob_grads - delta_row)).astype(BF16)
            value_part = nn(probs.astype(BF16), grad_rows)
            key_part = nn(score_grads, query_rows)
            if slot == 0:
                dv_acc[head] = value_part
                dk_acc[head] = key_part
            else:
                dv_acc[head] += value_part
                dk_acc[head] += key_part

    def arrived_pair(x, slot):
        arrived(x, slot)
        arrived(x, slot + 1)

    shift = one(origin(-1, 0)) + 2 * one(origin(0, -1))

    def query_step(number):
        step = lax.rem(number + shift, 4)
        for at, slot in ((0, 1), (2, 5), (3, 7)):

            @pl.when(step == at)
            def _():
                arrived_pair(K, slot)
                arrived_pair(V, slot)

        empty = ((step == 2) & jnp.logical_not(up_down[1])) | ((step == 3) & jnp.logical_not(up_down[-1]))
        pl.when(jnp.logical_not(empty))(lambda: query_side(1 + 2 * step, 2))

    query_side(0, 1)
    await_ahead(0)
    for x in (K, V):
        pl.when(exists(1, 0) & jnp.logical_not(at_origin))(lambda: copy_of(x, 0, 1, 0).start())
    await_ahead(1)
    for x in (K, V):
        pl.when(exists(0, 1) & jnp.logical_not(at_origin))(lambda: copy_of(x, 0, 0, 1).start())

    def send_all(x):
        send(x, 0, 1)
        send(x, 1, 0)
        send(x, 0, -1)
        send(x, -1, 0)
        pl.when(direct)(lambda: direct_copy(x).start())

    send_all(Q)
    forward_upper(K)
    forward_lower(K)
    forward_upper(V)
    forward_lower(V)
    query_step(0)
    send_all(G)
    query_step(1)
    forward_upper(Q)
    forward_lower(Q)
    query_step(2)
    forward_upper(G)
    forward_lower(G)

    await_ready(len(AHEAD), by_origin[(-1, 0)] | by_origin[(0, -1)])
    for x in (K, V):
        send(x, -1, 0, late=True)
        send(x, 0, -1, late=True)
        pass_on(x, 4, -1, in_turn(exists(-1, 1), origin(-1, 0), True))
    for x in (K, V):
        forward_lower(x, late=True)
    for x in (Q, G):
        send(x, -1, 0, late=True)
        send(x, 0, -1, late=True)
        pass_on(x, 4, -1, in_turn(exists(-1, 1), origin(-1, 0), True))
    query_step(3)

    for head in range(heads):
        log_total = as_row(run_max[head] + jnp.log2(run_sum[head]))
        delta = as_row(delta_col[head])
        for slot in range(9):
            stat_out[slot, head : head + 1] = log_total - bias[slot]
            stat_out[slot, heads + head : heads + head + 1] = delta

    def stat_copy(slot):
        lands = SLOT_OF[opposite(SLOTS[slot])]
        return pltpu.make_async_remote_copy(
            src_ref=stat_out.at[slot],
            dst_ref=stat_in.at[lands],
            send_sem=stat_send.at[slot],
            recv_sem=stat_recv.at[lands],
            device_id=device(*SLOTS[slot]),
            device_id_type=MESH,
        )

    await_ahead(2)
    await_ahead(3)
    await_ready(len(AHEAD), by_origin[(-1, -1)])
    for slot in range(1, 9):
        if_there(*SLOTS[slot])(lambda: stat_copy(slot).start())

    for x in (Q, G):
        forward_lower(x, late=True)

    for head in range(heads):
        results[0, head] = (dq_acc[head] * (scale / run_sum[head])).astype(BF16)
    out_copies = [
        pltpu.make_async_copy(results.at[i], out, out_sem.at[i])
        for i, out in enumerate((dq_ref, dk_ref, dv_ref))
    ]
    out_copies[0].start()

    key_side(0, 1, stat_out)

    def stat_arrived(slot):
        @if_there(*SLOTS[slot])
        def _():
            pltpu.make_async_copy(stat_in.at[slot], stat_in.at[slot], stat_recv.at[slot]).wait()

    for slot in (1, 3, 5, 7):
        stat_arrived(slot)
        stat_arrived(slot + 1)
        if slot != 3:
            arrived_pair(Q, slot)
            arrived_pair(G, slot)
        if slot < 5:
            key_side(slot, 2, stat_in)
        else:
            pl.when(up_down[1 if slot == 5 else -1])(lambda: key_side(slot, 2, stat_in))

    for head in range(heads):
        results[1, head] = (dk_acc[head] * scale).astype(BF16)
    out_copies[1].start()
    for head in range(heads):
        results[2, head] = dv_acc[head].astype(BF16)
    out_copies[2].start()

    for slot in range(1, 9):
        if_there(*SLOTS[slot])(lambda: stat_copy(slot).wait_send())
    for x in (K, V, Q, G):
        for offset in ((0, -1), (0, 1), (-1, 0), (1, 0)):
            if_there(*offset)(lambda: copy_of(x, 0, *offset).wait_send())
        for side in (-1, 1):
            if_there(side, -1)(lambda: copy_of(x, 3, side, 0).wait_send())
        if_there(-1, 1)(lambda: copy_of(x, 4, -1, 0).wait_send())
        pl.when(in_turn(exists(1, 1), origin(0, 0), False))(
            lambda: copy_of(x, 4, 1, 0).wait_send()
        )
        pl.when(direct)(lambda: direct_copy(x).wait_send())
    for copy in out_copies:
        copy.wait()


def settle(*refs):
    sources, targets, (semaphore, held) = refs[:3], refs[3:6], refs[6:]
    loads = [pltpu.make_async_copy(sources[i], held.at[i], semaphore.at[i]) for i in range(3)]
    stores = [pltpu.make_async_copy(held.at[i], targets[i], semaphore.at[3 + i]) for i in range(3)]
    for load in loads:
        load.start()
    for load, store in zip(loads, stores):
        load.wait()
        store.start()
    for store in stores:
        store.wait()


def body(sizes, queries, keys, values, grad_out, attn_out, window_mask):
    shape = queries.shape
    tile = (shape[2],) + shape[4:]
    heads, rows, depth = tile
    flat = [x.reshape(tile) for x in (queries, keys, values, grad_out, attn_out)]
    in_place = pl.BlockSpec(memory_space=pl.ANY)
    outs = pl.pallas_call(
        functools.partial(kernel, sizes),
        out_shape=[jax.ShapeDtypeStruct(tile, BF16)] * 3,
        in_specs=[in_place] * 6,
        out_specs=[in_place] * 3,
        scratch_shapes=[
            pltpu.SMEM(window_mask.shape, jnp.int32),
            pltpu.VMEM((3,) + tile, BF16),
            pltpu.VMEM((4, heads, 9, rows, depth), BF16),
            pltpu.VMEM(tile, BF16),
            pltpu.VMEM((9, 2 * heads, rows), F32),
            pltpu.VMEM((9, 2 * heads, rows), F32),
            pltpu.SMEM((9,), F32),
            pltpu.VMEM((heads, rows, 1), F32),
            pltpu.VMEM((heads, rows, 1), F32),
            pltpu.VMEM((heads, rows, 1), F32),
            pltpu.VMEM(tile, F32),
            pltpu.VMEM(tile, F32),
            pltpu.VMEM(tile, F32),
            pltpu.SemaphoreType.DMA((5,)),
            pltpu.SemaphoreType.DMA((4, 9)),
            pltpu.SemaphoreType.DMA((4, 9)),
            pltpu.SemaphoreType.DMA((9,)),
            pltpu.SemaphoreType.DMA((9,)),
            pltpu.SemaphoreType.REGULAR((len(AHEAD) + 1,)),
            pltpu.SemaphoreType.DMA,
            pltpu.SemaphoreType.DMA((3,)),
        ],
        compiler_params=pltpu.CompilerParams(
            collective_id=0, has_side_effects=True, vmem_limit_bytes=54 << 20
        ),
        name="tile_attention_backward",
    )(window_mask, *flat)
    outs = pl.pallas_call(
        settle,
        out_shape=[jax.ShapeDtypeStruct(tile, BF16)] * 3,
        in_specs=[in_place] * 3,
        out_specs=[in_place] * 3,
        scratch_shapes=[pltpu.SemaphoreType.DMA((6,)), pltpu.VMEM((3,) + tile, BF16)],
        compiler_params=pltpu.CompilerParams(vmem_limit_bytes=54 << 20),
        name="settle",
    )(*outs)
    return tuple(x.reshape(shape) for x in outs)


def solution(mesh):
    sizes = (mesh.shape["tm"], mesh.shape["height"])
    tiled = P("tm", "height", "dp", None, None, None)
    return jax.shard_map(
        functools.partial(body, sizes),
        mesh=mesh,
        in_specs=(tiled,) * 5 + (P("tm", "height", None, None),),
        out_specs=(tiled,) * 3,
        check_vma=False,
    )
```

```python
import functools

import jax
import jax.numpy as jnp
from jax import lax
from jax.experimental import pallas as pl
from jax.experimental.pallas import tpu as pltpu
from jax.sharding import PartitionSpec as P

MESH = pl.DeviceIdType.MESH
F32 = jnp.float32
BF16 = jnp.bfloat16
LOG2E = 1.4426950408889634
FAR = 1e30

SLOTS = ((0, 0), (-1, 0), (1, 0), (0, -1), (0, 1), (-1, 1), (1, 1), (-1, -1), (1, -1))
AHEAD = ((1, 0), (0, 1), (-1, 1), (1, 1))
SLOT_OF = {offset: slot for slot, offset in enumerate(SLOTS)}
K, V, Q, G = range(4)


def nt(a, b):
    return lax.dot_general(a, b, (((1,), (1,)), ((), ())), preferred_element_type=F32)


def nn(a, b):
    return lax.dot_general(a, b, (((1,), (0,)), ((), ())), preferred_element_type=F32)


def kernel(
    sizes,
    mask_ref,
    q_ref,
    k_ref,
    v_ref,
    g_ref,
    o_ref,
    dq_ref,
    dk_ref,
    dv_ref,
    mask,
    results,
    tiles,
    out_tile,
    stat_out,
    stat_in,
    bias,
    run_max,
    run_sum,
    delta_col,
    dq_acc,
    dk_acc,
    dv_acc,
    local_sem,
    send_sem,
    recv_sem,
    stat_send,
    stat_recv,
    ready,
    mask_sem,
    out_sem,
):
    n_t, n_h = sizes
    heads, rows, depth = q_ref.shape
    scale = depth**-0.5
    score_scale = scale * LOG2E
    t = lax.axis_index("tm")
    h = lax.axis_index("height")
    d = lax.axis_index("dp")
    along = {-1: t > 0, 1: t < n_t - 1}
    up_down = {-1: h > 0, 1: h < n_h - 1}

    def exists(side, dh):
        if side == 0:
            return up_down[dh]
        return along[side] if dh == 0 else along[side] & up_down[dh]

    def origin(side, dh):
        return (t + side == 0) & (h + dh == 0) & (d == 0)

    direct = (t == 0) & (h == 1) & (d == 0)

    def device(side, dh):
        return (t + side, h + dh, d)

    def if_there(side, dh):
        return pl.when(exists(side, dh))

    def opposite(offset):
        return (-offset[0], -offset[1])

    barrier = pltpu.get_barrier_semaphore()
    at_origin = origin(0, 0)
    by_origin = {offset: origin(*offset) for offset in ((-1, 0), (0, -1), (-1, -1))}
    near_origin = by_origin[(-1, 0)] | by_origin[(0, -1)] | by_origin[(-1, -1)]

    def signal(semaphore, offset, there):
        @pl.when(there)
        def _():
            pl.semaphore_signal(semaphore, inc=1, device_id=device(*offset), device_id_type=MESH)

    for offset in AHEAD:
        signal(barrier, offset, exists(*offset) & jnp.logical_not(at_origin))
    for offset, there in by_origin.items():
        signal(barrier, offset, there)

    sources = {K: k_ref, V: v_ref, Q: q_ref, G: g_ref}
    locals_ = [
        pltpu.make_async_copy(sources[x], tiles.at[x, :, 0], local_sem.at[x]) for x in (K, V, Q, G)
    ]
    locals_.append(pltpu.make_async_copy(o_ref, out_tile, local_sem.at[4]))
    mask_copy = pltpu.make_async_copy(mask_ref, mask, mask_sem)
    mask_copy.start()
    for copy in locals_:
        copy.start()

    def copy_of(x, from_slot, side, dh):
        own_side, own_dh = SLOTS[from_slot]
        lands = SLOT_OF[(own_side - side, own_dh - dh)]
        return pltpu.make_async_remote_copy(
            src_ref=sources[x] if from_slot == 0 else tiles.at[x, :, from_slot],
            dst_ref=tiles.at[x, :, lands],
            send_sem=send_sem.at[x, lands],
            recv_sem=recv_sem.at[x, lands],
            device_id=device(side, dh),
            device_id_type=MESH,
        )

    def direct_copy(x):
        slot = SLOT_OF[(-1, 1)]
        return pltpu.make_async_remote_copy(
            src_ref=sources[x],
            dst_ref=tiles.at[x, :, slot],
            send_sem=send_sem.at[x, 0],
            recv_sem=recv_sem.at[x, slot],
            device_id=device(1, -1),
            device_id_type=MESH,
        )

    def in_turn(there, at_origin, late):
        return there & (at_origin if late else jnp.logical_not(at_origin))

    def send(x, side, dh, late=False):
        there = exists(side, dh)
        if (side, dh) in ((-1, 0), (0, -1)):
            there = in_turn(there, origin(side, dh), late)
        pl.when(there)(lambda: copy_of(x, 0, side, dh).start())

    def arrived(x, slot, there=None):
        @pl.when(exists(*SLOTS[slot]) if there is None else there)
        def _():
            pltpu.make_async_copy(
                tiles.at[x, :, slot], tiles.at[x, :, slot], recv_sem.at[x, slot]
            ).wait()

    def pass_on(x, slot, side, there):
        pl.when(there)(lambda: copy_of(x, slot, side, 0).start())

    def forward_upper(x):
        arrived(x, 4, in_turn(exists(0, 1), at_origin, False))
        pass_on(x, 4, -1, in_turn(exists(-1, 1), origin(-1, 0), False))
        pass_on(x, 4, 1, in_turn(exists(1, 1), origin(0, 0), False))

    def forward_lower(x, late=False):
        arrived(x, 3, in_turn(exists(0, -1), origin(0, -1), late))
        for side in (-1, 1):
            pass_on(x, 3, side, in_turn(exists(side, -1), origin(0, -1), late))

    def one(there):
        return there.astype(jnp.int32)

    behind = one(along[-1]) + one(up_down[-1]) * (1 + one(along[-1]) + one(along[1]))
    expected = behind - one(near_origin) + 3 * one(at_origin)

    @pl.when(expected > 0)
    def _():
        pl.semaphore_wait(barrier, expected)

    for number, offset in enumerate(AHEAD):
        there = exists(*opposite(offset))
        if opposite(offset) in by_origin:
            there = there & jnp.logical_not(by_origin[opposite(offset)])
        signal(ready.at[number], opposite(offset), there)
        if offset != (-1, 1):
            signal(ready.at[len(AHEAD)], offset, at_origin)

    def await_ready(number, there):
        pl.when(there)(lambda: pl.semaphore_wait(ready.at[number], 1))

    def await_ahead(number):
        await_ready(number, exists(*AHEAD[number]) & jnp.logical_not(at_origin))

    for x in (K, V):
        send(x, 0, -1)
        send(x, -1, 0)
        pl.when(direct)(lambda: direct_copy(x).start())
        for offset in ((1, 0), (0, 1)):
            pl.when(at_origin)(lambda: copy_of(x, 0, *offset).start())

    mask_copy.wait()
    for slot, (side, dh) in enumerate(SLOTS):
        if slot == 0:
            bias[slot] = jnp.float32(0)
        else:
            chosen = mask[0, 0, 0, 9 * (side + 1) + 3 * (dh + 1) + 1] != 0
            bias[slot] = jnp.where(exists(side, dh) & chosen, jnp.float32(0), jnp.float32(-FAR))

    for slot in range(1, 9):

        @pl.when(jnp.logical_not(exists(*SLOTS[slot])))
        def _():
            stat_in[slot, :heads] = jnp.full((heads, rows), FAR, F32)
            stat_in[slot, heads:] = jnp.zeros((heads, rows), F32)

            def clear(x, carry):
                tiles[x, :, slot] = jnp.zeros((heads, rows, depth), BF16)
                return carry

            lax.fori_loop(0, 4, clear, 0)

    for copy in locals_:
        copy.wait()

    for head in range(heads):
        product = tiles[G, head, 0].astype(F32) * out_tile[head].astype(F32)
        delta_col[head] = jnp.sum(product, axis=1, keepdims=True)

    def as_row(column):
        return jnp.broadcast_to(column, (rows, 128)).T[:1]

    def query_side(slot, count):
        keys = count * rows
        if count == 2:
            lane = lax.broadcasted_iota(jnp.int32, (1, keys), 1)
            bias_row = jnp.where(lane < rows, bias[slot], bias[slot + 1])
        else:
            bias_row = bias[slot]
        for head in range(heads):
            key_rows = tiles[K, head, pl.ds(slot, count)].reshape(keys, depth)
            value_rows = tiles[V, head, pl.ds(slot, count)].reshape(keys, depth)
            scores = nt(tiles[Q, head, 0], key_rows) * score_scale + bias_row
            top = jnp.max(scores, axis=1, keepdims=True)
            if count == 2:
                old_max = run_max[head]
                top = jnp.maximum(old_max, top)
                decay = jnp.exp2(old_max - top)
            probs = jnp.exp2(scores - top)
            total = jnp.sum(probs, axis=1, keepdims=True)
            prob_grads = nt(tiles[G, head, 0], value_rows)
            score_grads = (probs * (prob_grads - delta_col[head])).astype(BF16)
            grads = nn(score_grads, key_rows)
            run_max[head] = top
            if count == 2:
                run_sum[head] = run_sum[head] * decay + total
                dq_acc[head] = dq_acc[head] * decay + grads
            else:
                run_sum[head] = total
                dq_acc[head] = grads

    def key_side(slot, count, stats):
        queries = count * rows
        for head in range(heads):
            query_rows = tiles[Q, head, pl.ds(slot, count)].reshape(queries, depth)
            grad_rows = tiles[G, head, pl.ds(slot, count)].reshape(queries, depth)
            log_row = [stats[slot + i, head : head + 1] for i in range(count)]
            delta_row = [stats[slot + i, heads + head : heads + head + 1] for i in range(count)]
            if count == 2:
                log_row, delta_row = jnp.concatenate(log_row, 1), jnp.concatenate(delta_row, 1)
            else:
                log_row, delta_row = log_row[0], delta_row[0]
            probs = jnp.exp2(nt(tiles[K, head, 0], query_rows) * score_scale - log_row)
            prob_grads = nt(tiles[V, head, 0], grad_rows)
            score_grads = (probs * (prob_grads - delta_row)).astype(BF16)
            value_part = nn(probs.astype(BF16), grad_rows)
            key_part = nn(score_grads, query_rows)
            if count == 1:
                dv_acc[head] = value_part
                dk_acc[head] = key_part
            else:
                dv_acc[head] += value_part
                dk_acc[head] += key_part

    def arrived_pair(x, slot):
        arrived(x, slot)
        arrived(x, slot + 1)

    shift = one(origin(-1, 0)) + 2 * one(origin(0, -1)) + 2 * one(at_origin)

    def is_empty(step):
        upper = (step == 2) & jnp.logical_not(up_down[1])
        return upper | ((step == 3) & jnp.logical_not(up_down[-1]))

    def query_step(number):
        step = lax.rem(number + shift, 4)
        for at, slot in ((0, 1), (2, 5), (3, 7)):

            @pl.when(step == at)
            def _():
                arrived_pair(K, slot)
                arrived_pair(V, slot)

        pl.when(jnp.logical_not(is_empty(step)))(lambda: query_side(1 + 2 * step, 2))

    query_side(0, 1)
    await_ahead(0)
    for x in (K, V):
        pl.when(exists(1, 0) & jnp.logical_not(at_origin))(lambda: copy_of(x, 0, 1, 0).start())
    await_ahead(1)
    for x in (K, V):
        pl.when(exists(0, 1) & jnp.logical_not(at_origin))(lambda: copy_of(x, 0, 0, 1).start())

    def send_all(x):
        for offset in ((0, 1), (1, 0)):
            there = exists(*offset)
            if x == G:
                there = in_turn(there, at_origin, False)
            pl.when(there)(lambda: copy_of(x, 0, *offset).start())
        send(x, 0, -1)
        send(x, -1, 0)
        pl.when(direct)(lambda: direct_copy(x).start())

    send_all(Q)

    @pl.when(at_origin)
    def _():
        copy_of(G, 0, 0, 1).start()
        copy_of(G, 0, 1, 0).start()

    forward_upper(K)
    forward_lower(K)
    forward_upper(V)
    forward_lower(V)
    query_step(0)
    send_all(G)
    query_step(1)
    forward_upper(Q)
    forward_lower(Q)
    query_step(2)
    forward_upper(G)
    forward_lower(G)

    await_ready(len(AHEAD), by_origin[(-1, 0)] | by_origin[(0, -1)])
    for x in (K, V):
        send(x, -1, 0, late=True)
        send(x, 0, -1, late=True)
        pass_on(x, 4, -1, in_turn(exists(-1, 1), origin(-1, 0), True))
    for x in (K, V):
        forward_lower(x, late=True)
        arrived(x, 4, at_origin)
    for x in (Q, G):
        send(x, -1, 0, late=True)
        send(x, 0, -1, late=True)
        pass_on(x, 4, -1, in_turn(exists(-1, 1), origin(-1, 0), True))
    query_step(3)

    for head in range(heads):
        log_total = as_row(run_max[head] + jnp.log2(run_sum[head]))
        delta = as_row(delta_col[head])
        for slot in range(9):
            stat_out[slot, head : head + 1] = log_total - bias[slot]
            stat_out[slot, heads + head : heads + head + 1] = delta

    def stat_copy(slot):
        lands = SLOT_OF[opposite(SLOTS[slot])]
        return pltpu.make_async_remote_copy(
            src_ref=stat_out.at[slot],
            dst_ref=stat_in.at[lands],
            send_sem=stat_send.at[slot],
            recv_sem=stat_recv.at[lands],
            device_id=device(*SLOTS[slot]),
            device_id_type=MESH,
        )

    await_ahead(2)
    await_ahead(3)
    await_ready(len(AHEAD), by_origin[(-1, -1)])
    for slot in range(1, 9):
        if_there(*SLOTS[slot])(lambda: stat_copy(slot).start())

    for x in (Q, G):
        forward_lower(x, late=True)
        arrived(x, 4, at_origin)

    for head in range(heads):
        results[0, head] = (dq_acc[head] * (scale / run_sum[head])).astype(BF16)
    out_copies = [
        pltpu.make_async_copy(results.at[i], out, out_sem.at[i])
        for i, out in enumerate((dq_ref, dk_ref, dv_ref))
    ]
    out_copies[0].start()

    key_side(0, 1, stat_out)

    def stat_arrived(slot):
        @if_there(*SLOTS[slot])
        def _():
            pltpu.make_async_copy(stat_in.at[slot], stat_in.at[slot], stat_recv.at[slot]).wait()

    def key_step(number, carry):
        step = lax.rem(number + shift, 4)
        for at, slot in enumerate((1, 3, 5, 7)):

            @pl.when(step == at)
            def _():
                stat_arrived(slot)
                stat_arrived(slot + 1)
                if slot != 3:
                    arrived_pair(Q, slot)
                    arrived_pair(G, slot)

        pl.when(jnp.logical_not(is_empty(step)))(lambda: key_side(1 + 2 * step, 2, stat_in))
        return carry

    lax.fori_loop(0, 4, key_step, 0)

    for head in range(heads):
        results[1, head] = (dk_acc[head] * scale).astype(BF16)
    out_copies[1].start()
    for head in range(heads):
        results[2, head] = dv_acc[head].astype(BF16)
    out_copies[2].start()

    for slot in range(1, 9):
        if_there(*SLOTS[slot])(lambda: stat_copy(slot).wait_send())
    for x in (K, V, Q, G):
        for offset in ((0, -1), (0, 1), (-1, 0), (1, 0)):
            if_there(*offset)(lambda: copy_of(x, 0, *offset).wait_send())
        for side in (-1, 1):
            if_there(side, -1)(lambda: copy_of(x, 3, side, 0).wait_send())
        if_there(-1, 1)(lambda: copy_of(x, 4, -1, 0).wait_send())
        pl.when(in_turn(exists(1, 1), origin(0, 0), False))(
            lambda: copy_of(x, 4, 1, 0).wait_send()
        )
        pl.when(direct)(lambda: direct_copy(x).wait_send())
    for copy in out_copies:
        copy.wait()


def settle(*refs):
    sources, targets, (semaphore, held) = refs[:3], refs[3:6], refs[6:]
    loads = [pltpu.make_async_copy(sources[i], held.at[i], semaphore.at[i]) for i in range(3)]
    stores = [pltpu.make_async_copy(held.at[i], targets[i], semaphore.at[3 + i]) for i in range(3)]
    for load in loads:
        load.start()
    for load, store in zip(loads, stores):
        load.wait()
        store.start()
    for store in stores:
        store.wait()


def body(sizes, queries, keys, values, grad_out, attn_out, window_mask):
    shape = queries.shape
    tile = (shape[2],) + shape[4:]
    heads, rows, depth = tile
    flat = [x.reshape(tile) for x in (queries, keys, values, grad_out, attn_out)]
    in_place = pl.BlockSpec(memory_space=pl.ANY)
    outs = pl.pallas_call(
        functools.partial(kernel, sizes),
        out_shape=[jax.ShapeDtypeStruct(tile, BF16)] * 3,
        in_specs=[in_place] * 6,
        out_specs=[in_place] * 3,
        scratch_shapes=[
            pltpu.SMEM(window_mask.shape, jnp.int32),
            pltpu.VMEM((3,) + tile, BF16),
            pltpu.VMEM((4, heads, 9, rows, depth), BF16),
            pltpu.VMEM(tile, BF16),
            pltpu.VMEM((9, 2 * heads, rows), F32),
            pltpu.VMEM((9, 2 * heads, rows), F32),
            pltpu.SMEM((9,), F32),
            pltpu.VMEM((heads, rows, 1), F32),
            pltpu.VMEM((heads, rows, 1), F32),
            pltpu.VMEM((heads, rows, 1), F32),
            pltpu.VMEM(tile, F32),
            pltpu.VMEM(tile, F32),
            pltpu.VMEM(tile, F32),
            pltpu.SemaphoreType.DMA((5,)),
            pltpu.SemaphoreType.DMA((4, 9)),
            pltpu.SemaphoreType.DMA((4, 9)),
            pltpu.SemaphoreType.DMA((9,)),
            pltpu.SemaphoreType.DMA((9,)),
            pltpu.SemaphoreType.REGULAR((len(AHEAD) + 1,)),
            pltpu.SemaphoreType.DMA,
            pltpu.SemaphoreType.DMA((3,)),
        ],
        compiler_params=pltpu.CompilerParams(
            collective_id=0, has_side_effects=True, vmem_limit_bytes=54 << 20
        ),
        name="tile_attention_backward",
    )(window_mask, *flat)
    outs = pl.pallas_call(
        settle,
        out_shape=[jax.ShapeDtypeStruct(tile, BF16)] * 3,
        in_specs=[in_place] * 3,
        out_specs=[in_place] * 3,
        scratch_shapes=[pltpu.SemaphoreType.DMA((6,)), pltpu.VMEM((3,) + tile, BF16)],
        compiler_params=pltpu.CompilerParams(vmem_limit_bytes=54 << 20),
        name="settle",
    )(*outs)
    return tuple(x.reshape(shape) for x in outs)


def solution(mesh):
    sizes = (mesh.shape["tm"], mesh.shape["height"])
    tiled = P("tm", "height", "dp", None, None, None)
    return jax.shard_map(
        functools.partial(body, sizes),
        mesh=mesh,
        in_specs=(tiled,) * 5 + (P("tm", "height", None, None),),
        out_specs=(tiled,) * 3,
        check_vma=False,
    )
```

```python
import functools

import jax
import jax.numpy as jnp
from jax import lax
from jax.experimental import pallas as pl
from jax.experimental.pallas import tpu as pltpu
from jax.sharding import PartitionSpec as P

MESH = pl.DeviceIdType.MESH
F32 = jnp.float32
BF16 = jnp.bfloat16
LOG2E = 1.4426950408889634
FAR = 1e30

SLOTS = ((0, 0), (-1, 0), (1, 0), (0, -1), (0, 1), (-1, 1), (1, 1), (-1, -1), (1, -1))
AHEAD = ((0, 1), (-1, 1), (1, 1))
SLOT_OF = {offset: slot for slot, offset in enumerate(SLOTS)}
K, V, Q, G = range(4)


def nt(a, b):
    return lax.dot_general(a, b, (((1,), (1,)), ((), ())), preferred_element_type=F32)


def nn(a, b):
    return lax.dot_general(a, b, (((1,), (0,)), ((), ())), preferred_element_type=F32)


def kernel(
    sizes,
    mask_ref,
    q_ref,
    k_ref,
    v_ref,
    g_ref,
    o_ref,
    dq_ref,
    dk_ref,
    dv_ref,
    mask,
    results,
    tiles,
    out_tile,
    stat_out,
    stat_in,
    bias,
    held_scores,
    run_max,
    run_sum,
    delta_col,
    dq_acc,
    dk_acc,
    dv_acc,
    local_sem,
    send_sem,
    recv_sem,
    stat_send,
    stat_recv,
    ready,
    mask_sem,
    out_sem,
):
    n_t, n_h = sizes
    heads, rows, depth = q_ref.shape
    scale = depth**-0.5
    score_scale = scale * LOG2E
    t = lax.axis_index("tm")
    h = lax.axis_index("height")
    d = lax.axis_index("dp")
    along = {-1: t > 0, 1: t < n_t - 1}
    up_down = {-1: h > 0, 1: h < n_h - 1}

    def exists(side, dh):
        if side == 0:
            return up_down[dh]
        return along[side] if dh == 0 else along[side] & up_down[dh]

    def origin(side, dh):
        return (t + side == 0) & (h + dh == 0) & (d == 0)

    direct = (t == 0) & (h == 1) & (d == 0)

    def device(side, dh):
        return (t + side, h + dh, d)

    def if_there(side, dh):
        return pl.when(exists(side, dh))

    def opposite(offset):
        return (-offset[0], -offset[1])

    barrier = pltpu.get_barrier_semaphore()
    at_origin = origin(0, 0)
    by_origin = {offset: origin(*offset) for offset in ((-1, 0), (0, -1), (-1, -1))}
    near_origin = by_origin[(-1, 0)] | by_origin[(0, -1)] | by_origin[(-1, -1)]

    def signal(semaphore, offset, there):
        @pl.when(there)
        def _():
            pl.semaphore_signal(semaphore, inc=1, device_id=device(*offset), device_id_type=MESH)

    for offset in AHEAD + ((-1, 0), (1, 0)):
        signal(barrier, offset, exists(*offset) & jnp.logical_not(at_origin))
    for offset in ((0, -1), (-1, -1)):
        signal(barrier, offset, by_origin[offset])

    sources = {K: k_ref, V: v_ref, Q: q_ref, G: g_ref}
    locals_ = [
        pltpu.make_async_copy(sources[x], tiles.at[x, :, 0], local_sem.at[x]) for x in (K, V, Q, G)
    ]
    locals_.append(pltpu.make_async_copy(o_ref, out_tile, local_sem.at[4]))
    mask_copy = pltpu.make_async_copy(mask_ref, mask, mask_sem)
    mask_copy.start()
    for copy in locals_:
        copy.start()

    def copy_of(x, from_slot, side, dh):
        own_side, own_dh = SLOTS[from_slot]
        lands = SLOT_OF[(own_side - side, own_dh - dh)]
        return pltpu.make_async_remote_copy(
            src_ref=sources[x] if from_slot == 0 else tiles.at[x, :, from_slot],
            dst_ref=tiles.at[x, :, lands],
            send_sem=send_sem.at[x, lands],
            recv_sem=recv_sem.at[x, lands],
            device_id=device(side, dh),
            device_id_type=MESH,
        )

    def direct_copy(x):
        slot = SLOT_OF[(-1, 1)]
        return pltpu.make_async_remote_copy(
            src_ref=sources[x],
            dst_ref=tiles.at[x, :, slot],
            send_sem=send_sem.at[x, 0],
            recv_sem=recv_sem.at[x, slot],
            device_id=device(1, -1),
            device_id_type=MESH,
        )

    def in_turn(there, at_origin, late):
        return there & (at_origin if late else jnp.logical_not(at_origin))

    def send(x, side, dh, late=False):
        there = exists(side, dh)
        if (side, dh) in ((-1, 0), (0, -1)):
            there = in_turn(there, origin(side, dh), late)
        pl.when(there)(lambda: copy_of(x, 0, side, dh).start())

    def arrived(x, slot, there=None):
        @pl.when(exists(*SLOTS[slot]) if there is None else there)
        def _():
            pltpu.make_async_copy(
                tiles.at[x, :, slot], tiles.at[x, :, slot], recv_sem.at[x, slot]
            ).wait()

    def pass_on(x, slot, side, there):
        pl.when(there)(lambda: copy_of(x, slot, side, 0).start())

    def forward_upper(x):
        arrived(x, 4, in_turn(exists(0, 1), at_origin, False))
        pass_on(x, 4, -1, in_turn(exists(-1, 1), origin(-1, 0), False))
        pass_on(x, 4, 1, in_turn(exists(1, 1), origin(0, 0), False))

    def forward_lower(x, late=False):
        arrived(x, 3, in_turn(exists(0, -1), origin(0, -1), late))
        for side in (-1, 1):
            pass_on(x, 3, side, in_turn(exists(side, -1), origin(0, -1), late))

    def one(there):
        return there.astype(jnp.int32)

    sides = one(along[-1]) + one(along[1])
    expected = sides + one(up_down[-1]) * (1 + sides) - one(near_origin) + 2 * one(at_origin)

    @pl.when(expected > 0)
    def _():
        pl.semaphore_wait(barrier, expected)

    for number, offset in enumerate(AHEAD):
        there = exists(*opposite(offset))
        if opposite(offset) in by_origin:
            there = there & jnp.logical_not(by_origin[opposite(offset)])
        signal(ready.at[number], opposite(offset), there)
    for offset in ((1, 0), (0, 1), (1, 1)):
        signal(ready.at[len(AHEAD)], offset, at_origin)

    def await_ready(number, there):
        pl.when(there)(lambda: pl.semaphore_wait(ready.at[number], 1))

    def await_ahead(number):
        await_ready(number, exists(*AHEAD[number]) & jnp.logical_not(at_origin))

    for x in (K, V):
        send(x, 0, -1)
        send(x, -1, 0)
        send(x, 1, 0)
        pl.when(direct)(lambda: direct_copy(x).start())
        pl.when(at_origin)(lambda: copy_of(x, 0, 0, 1).start())

    mask_copy.wait()
    for slot, (side, dh) in enumerate(SLOTS):
        if slot == 0:
            bias[slot] = jnp.float32(0)
        else:
            chosen = mask[0, 0, 0, 9 * (side + 1) + 3 * (dh + 1) + 1] != 0
            bias[slot] = jnp.where(exists(side, dh) & chosen, jnp.float32(0), jnp.float32(-FAR))

    for slot in range(1, 9):

        @pl.when(jnp.logical_not(exists(*SLOTS[slot])))
        def _():
            stat_in[slot, :heads] = jnp.full((heads, rows), FAR, F32)
            stat_in[slot, heads:] = jnp.zeros((heads, rows), F32)

            def clear(x, carry):
                tiles[x, :, slot] = jnp.zeros((heads, rows, depth), BF16)
                return carry

            lax.fori_loop(0, 4, clear, 0)

    for copy in locals_:
        copy.wait()

    for head in range(heads):
        product = tiles[G, head, 0].astype(F32) * out_tile[head].astype(F32)
        delta_col[head] = jnp.sum(product, axis=1, keepdims=True)

    def as_row(column):
        return jnp.broadcast_to(column, (rows, 128)).T[:1]

    def score_side(slot, count, index):
        keys = count * rows
        if count == 2:
            lane = lax.broadcasted_iota(jnp.int32, (1, keys), 1)
            bias_row = jnp.where(lane < rows, bias[slot], bias[slot + 1])
        else:
            bias_row = bias[slot]
        for head in range(heads):
            key_rows = tiles[K, head, pl.ds(slot, count)].reshape(keys, depth)
            scores = nt(tiles[Q, head, 0], key_rows) * score_scale + bias_row
            held_scores[index, head, :, :keys] = scores
            top = jnp.max(scores, axis=1, keepdims=True)
            if count == 2:
                old_max = run_max[head]
                top = jnp.maximum(old_max, top)
            total = jnp.sum(jnp.exp2(scores - top), axis=1, keepdims=True)
            if count == 2:
                total = run_sum[head] * jnp.exp2(old_max - top) + total
            run_max[head] = top
            run_sum[head] = total

    def query_side(slot, count, index):
        keys = count * rows
        for head in range(heads):
            key_rows = tiles[K, head, pl.ds(slot, count)].reshape(keys, depth)
            value_rows = tiles[V, head, pl.ds(slot, count)].reshape(keys, depth)
            probs = jnp.exp2(held_scores[index, head, :, :keys] - run_max[head])
            prob_grads = nt(tiles[G, head, 0], value_rows)
            score_grads = (probs * (prob_grads - delta_col[head])).astype(BF16)
            grads = nn(score_grads, key_rows)
            if count == 2:
                dq_acc[head] += grads
            else:
                dq_acc[head] = grads

    def key_side(slot, count, stats):
        queries = count * rows
        for head in range(heads):
            query_rows = tiles[Q, head, pl.ds(slot, count)].reshape(queries, depth)
            grad_rows = tiles[G, head, pl.ds(slot, count)].reshape(queries, depth)
            log_row = [stats[slot + i, head : head + 1] for i in range(count)]
            delta_row = [stats[slot + i, heads + head : heads + head + 1] for i in range(count)]
            if count == 2:
                log_row, delta_row = jnp.concatenate(log_row, 1), jnp.concatenate(delta_row, 1)
            else:
                log_row, delta_row = log_row[0], delta_row[0]
            probs = jnp.exp2(nt(tiles[K, head, 0], query_rows) * score_scale - log_row)
            prob_grads = nt(tiles[V, head, 0], grad_rows)
            score_grads = (probs * (prob_grads - delta_row)).astype(BF16)
            value_part = nn(probs.astype(BF16), grad_rows)
            key_part = nn(score_grads, query_rows)
            if count == 1:
                dv_acc[head] = value_part
                dk_acc[head] = key_part
            else:
                dv_acc[head] += value_part
                dk_acc[head] += key_part

    def arrived_pair(x, slot):
        arrived(x, slot)
        arrived(x, slot + 1)

    shift = one(origin(-1, 0)) + 2 * one(origin(0, -1)) + 2 * one(at_origin)

    def is_empty(step):
        upper = (step == 2) & jnp.logical_not(up_down[1])
        return upper | ((step == 3) & jnp.logical_not(up_down[-1]))

    def step_of(x, side, number):
        step = lax.rem(number + shift, 4)
        for at, slot in ((0, 1), (2, 5), (3, 7)):
            pl.when(step == at)(lambda: arrived_pair(x, slot))
        pl.when(jnp.logical_not(is_empty(step)))(lambda: side(1 + 2 * step, 2, 1 + step))

    def score_step(number):
        step_of(K, score_side, number)

    def query_step(number):
        step_of(V, query_side, number)

    score_side(0, 1, 0)
    await_ahead(0)
    for x in (K, V):
        pl.when(exists(0, 1) & jnp.logical_not(at_origin))(lambda: copy_of(x, 0, 0, 1).start())

    def send_all(x):
        for offset in ((0, 1), (1, 0)):
            there = exists(*offset)
            if x == G:
                there = in_turn(there, at_origin, False)
            pl.when(there)(lambda: copy_of(x, 0, *offset).start())
        send(x, 0, -1)
        send(x, -1, 0)
        pl.when(direct)(lambda: direct_copy(x).start())

    send_all(Q)

    @pl.when(at_origin)
    def _():
        copy_of(G, 0, 0, 1).start()
        copy_of(G, 0, 1, 0).start()

    forward_upper(K)
    forward_lower(K)
    score_step(0)
    score_step(1)
    forward_upper(V)
    forward_lower(V)
    send_all(G)
    score_step(2)

    await_ready(len(AHEAD), by_origin[(-1, 0)] | by_origin[(0, -1)])
    for x in (K, V):
        send(x, -1, 0, late=True)
        send(x, 0, -1, late=True)
        pass_on(x, 4, -1, in_turn(exists(-1, 1), origin(-1, 0), True))
    forward_lower(K, late=True)
    arrived(K, 4, at_origin)
    score_step(3)

    for head in range(heads):
        run_max[head] += jnp.log2(run_sum[head])
    for head in range(heads):
        log_total = as_row(run_max[head])
        delta = as_row(delta_col[head])
        for slot in range(9):
            stat_out[slot, head : head + 1] = log_total - bias[slot]
            stat_out[slot, heads + head : heads + head + 1] = delta

    def stat_copy(slot):
        lands = SLOT_OF[opposite(SLOTS[slot])]
        return pltpu.make_async_remote_copy(
            src_ref=stat_out.at[slot],
            dst_ref=stat_in.at[lands],
            send_sem=stat_send.at[slot],
            recv_sem=stat_recv.at[lands],
            device_id=device(*SLOTS[slot]),
            device_id_type=MESH,
        )

    await_ahead(1)
    await_ahead(2)
    await_ready(len(AHEAD), by_origin[(-1, -1)])
    for slot in range(1, 9):
        if_there(*SLOTS[slot])(lambda: stat_copy(slot).start())

    forward_lower(V, late=True)
    arrived(V, 4, at_origin)
    forward_upper(Q)
    forward_lower(Q)
    query_side(0, 1, 0)
    query_step(0)
    forward_upper(G)
    forward_lower(G)
    for x in (Q, G):
        send(x, -1, 0, late=True)
        send(x, 0, -1, late=True)
        pass_on(x, 4, -1, in_turn(exists(-1, 1), origin(-1, 0), True))
    query_step(1)
    query_step(2)
    query_step(3)
    for x in (Q, G):
        forward_lower(x, late=True)
        arrived(x, 4, at_origin)

    for head in range(heads):
        results[0, head] = (dq_acc[head] * scale).astype(BF16)
    out_copies = [
        pltpu.make_async_copy(results.at[i], out, out_sem.at[i])
        for i, out in enumerate((dq_ref, dk_ref, dv_ref))
    ]
    out_copies[0].start()

    key_side(0, 1, stat_out)

    def stat_arrived(slot):
        @if_there(*SLOTS[slot])
        def _():
            pltpu.make_async_copy(stat_in.at[slot], stat_in.at[slot], stat_recv.at[slot]).wait()

    def key_step(number, carry):
        step = lax.rem(number + shift, 4)
        for at, slot in enumerate((1, 3, 5, 7)):

            @pl.when(step == at)
            def _():
                stat_arrived(slot)
                stat_arrived(slot + 1)
                if slot != 3:
                    arrived_pair(Q, slot)
                    arrived_pair(G, slot)

        pl.when(jnp.logical_not(is_empty(step)))(lambda: key_side(1 + 2 * step, 2, stat_in))
        return carry

    lax.fori_loop(0, 4, key_step, 0)

    for head in range(heads):
        results[1, head] = (dk_acc[head] * scale).astype(BF16)
    out_copies[1].start()
    for head in range(heads):
        results[2, head] = dv_acc[head].astype(BF16)
    out_copies[2].start()

    for slot in range(1, 9):
        if_there(*SLOTS[slot])(lambda: stat_copy(slot).wait_send())
    for x in (K, V, Q, G):
        for offset in ((0, -1), (0, 1), (-1, 0), (1, 0)):
            if_there(*offset)(lambda: copy_of(x, 0, *offset).wait_send())
        for side in (-1, 1):
            if_there(side, -1)(lambda: copy_of(x, 3, side, 0).wait_send())
        if_there(-1, 1)(lambda: copy_of(x, 4, -1, 0).wait_send())
        pl.when(in_turn(exists(1, 1), origin(0, 0), False))(
            lambda: copy_of(x, 4, 1, 0).wait_send()
        )
        pl.when(direct)(lambda: direct_copy(x).wait_send())
    for copy in out_copies:
        copy.wait()


def settle(*refs):
    sources, targets, (semaphore, held) = refs[:3], refs[3:6], refs[6:]
    loads = [pltpu.make_async_copy(sources[i], held.at[i], semaphore.at[i]) for i in range(3)]
    stores = [pltpu.make_async_copy(held.at[i], targets[i], semaphore.at[3 + i]) for i in range(3)]
    for load in loads:
        load.start()
    for load, store in zip(loads, stores):
        load.wait()
        store.start()
    for store in stores:
        store.wait()


def body(sizes, queries, keys, values, grad_out, attn_out, window_mask):
    shape = queries.shape
    tile = (shape[2],) + shape[4:]
    heads, rows, depth = tile
    flat = [x.reshape(tile) for x in (queries, keys, values, grad_out, attn_out)]
    in_place = pl.BlockSpec(memory_space=pl.ANY)
    outs = pl.pallas_call(
        functools.partial(kernel, sizes),
        out_shape=[jax.ShapeDtypeStruct(tile, BF16)] * 3,
        in_specs=[in_place] * 6,
        out_specs=[in_place] * 3,
        scratch_shapes=[
            pltpu.SMEM(window_mask.shape, jnp.int32),
            pltpu.VMEM((3,) + tile, BF16),
            pltpu.VMEM((4, heads, 9, rows, depth), BF16),
            pltpu.VMEM(tile, BF16),
            pltpu.VMEM((9, 2 * heads, rows), F32),
            pltpu.VMEM((9, 2 * heads, rows), F32),
            pltpu.SMEM((9,), F32),
            pltpu.VMEM((5, heads, rows, 2 * rows), F32),
            pltpu.VMEM((heads, rows, 1), F32),
            pltpu.VMEM((heads, rows, 1), F32),
            pltpu.VMEM((heads, rows, 1), F32),
            pltpu.VMEM(tile, F32),
            pltpu.VMEM(tile, F32),
            pltpu.VMEM(tile, F32),
            pltpu.SemaphoreType.DMA((5,)),
            pltpu.SemaphoreType.DMA((4, 9)),
            pltpu.SemaphoreType.DMA((4, 9)),
            pltpu.SemaphoreType.DMA((9,)),
            pltpu.SemaphoreType.DMA((9,)),
            pltpu.SemaphoreType.REGULAR((len(AHEAD) + 1,)),
            pltpu.SemaphoreType.DMA,
            pltpu.SemaphoreType.DMA((3,)),
        ],
        compiler_params=pltpu.CompilerParams(
            collective_id=0, has_side_effects=True, vmem_limit_bytes=54 << 20
        ),
        name="tile_attention_backward",
    )(window_mask, *flat)
    outs = pl.pallas_call(
        settle,
        out_shape=[jax.ShapeDtypeStruct(tile, BF16)] * 3,
        in_specs=[in_place] * 3,
        out_specs=[in_place] * 3,
        scratch_shapes=[pltpu.SemaphoreType.DMA((6,)), pltpu.VMEM((3,) + tile, BF16)],
        compiler_params=pltpu.CompilerParams(vmem_limit_bytes=54 << 20),
        name="settle",
    )(*outs)
    return tuple(x.reshape(shape) for x in outs)


def solution(mesh):
    sizes = (mesh.shape["tm"], mesh.shape["height"])
    tiled = P("tm", "height", "dp", None, None, None)
    return jax.shard_map(
        functools.partial(body, sizes),
        mesh=mesh,
        in_specs=(tiled,) * 5 + (P("tm", "height", None, None),),
        out_specs=(tiled,) * 3,
        check_vma=False,
    )
```

```python
import functools

import jax
import jax.numpy as jnp
from jax import lax
from jax.experimental import pallas as pl
from jax.experimental.pallas import tpu as pltpu
from jax.sharding import PartitionSpec as P

MESH = pl.DeviceIdType.MESH
F32 = jnp.float32
BF16 = jnp.bfloat16
LOG2E = 1.4426950408889634
FAR = 1e30

SLOTS = ((0, 0), (-1, 0), (1, 0), (0, -1), (0, 1), (-1, 1), (1, 1), (-1, -1), (1, -1))
AHEAD = ((0, 1), (-1, 1), (1, 1))
SLOT_OF = {offset: slot for slot, offset in enumerate(SLOTS)}
K, V, Q, G = range(4)


def nt(a, b):
    return lax.dot_general(a, b, (((1,), (1,)), ((), ())), preferred_element_type=F32)


def nn(a, b):
    return lax.dot_general(a, b, (((1,), (0,)), ((), ())), preferred_element_type=F32)


def kernel(
    sizes,
    mask_ref,
    q_ref,
    k_ref,
    v_ref,
    g_ref,
    o_ref,
    dq_ref,
    dk_ref,
    dv_ref,
    mask,
    results,
    tiles,
    out_tile,
    stat_out,
    stat_in,
    bias,
    held_scores,
    run_max,
    run_sum,
    delta_col,
    dq_acc,
    dk_acc,
    dv_acc,
    local_sem,
    send_sem,
    recv_sem,
    stat_send,
    stat_recv,
    ready,
    mask_sem,
    out_sem,
):
    n_t, n_h = sizes
    heads, rows, depth = q_ref.shape
    scale = depth**-0.5
    score_scale = scale * LOG2E
    t = lax.axis_index("tm")
    h = lax.axis_index("height")
    d = lax.axis_index("dp")
    along = {-1: t > 0, 1: t < n_t - 1}
    up_down = {-1: h > 0, 1: h < n_h - 1}

    def exists(side, dh):
        if side == 0:
            return up_down[dh]
        return along[side] if dh == 0 else along[side] & up_down[dh]

    def origin(side, dh):
        return (t + side == 0) & (h + dh == 0) & (d == 0)

    direct = (t == 0) & (h == 1) & (d == 0)

    def device(side, dh):
        return (t + side, h + dh, d)

    def if_there(side, dh):
        return pl.when(exists(side, dh))

    def opposite(offset):
        return (-offset[0], -offset[1])

    barrier = pltpu.get_barrier_semaphore()
    at_origin = origin(0, 0)
    by_origin = {offset: origin(*offset) for offset in ((-1, 0), (0, -1), (-1, -1))}
    near_origin = by_origin[(-1, 0)] | by_origin[(0, -1)] | by_origin[(-1, -1)]

    def signal(semaphore, offset, there):
        @pl.when(there)
        def _():
            pl.semaphore_signal(semaphore, inc=1, device_id=device(*offset), device_id_type=MESH)

    for offset in AHEAD + ((-1, 0), (1, 0)):
        signal(barrier, offset, exists(*offset) & jnp.logical_not(at_origin))
    for offset in ((0, -1), (-1, -1)):
        signal(barrier, offset, by_origin[offset])

    sources = {K: k_ref, V: v_ref, Q: q_ref, G: g_ref}
    locals_ = [
        pltpu.make_async_copy(sources[x], tiles.at[x, :, 0], local_sem.at[x]) for x in (K, V, Q, G)
    ]
    locals_.append(pltpu.make_async_copy(o_ref, out_tile, local_sem.at[4]))
    mask_copy = pltpu.make_async_copy(mask_ref, mask, mask_sem)
    mask_copy.start()
    for copy in locals_:
        copy.start()

    def copy_of(x, from_slot, side, dh):
        own_side, own_dh = SLOTS[from_slot]
        lands = SLOT_OF[(own_side - side, own_dh - dh)]
        return pltpu.make_async_remote_copy(
            src_ref=sources[x] if from_slot == 0 else tiles.at[x, :, from_slot],
            dst_ref=tiles.at[x, :, lands],
            send_sem=send_sem.at[x, lands],
            recv_sem=recv_sem.at[x, lands],
            device_id=device(side, dh),
            device_id_type=MESH,
        )

    def direct_copy(x):
        slot = SLOT_OF[(-1, 1)]
        return pltpu.make_async_remote_copy(
            src_ref=sources[x],
            dst_ref=tiles.at[x, :, slot],
            send_sem=send_sem.at[x, 0],
            recv_sem=recv_sem.at[x, slot],
            device_id=device(1, -1),
            device_id_type=MESH,
        )

    def in_turn(there, at_origin, late):
        return there & (at_origin if late else jnp.logical_not(at_origin))

    def send(x, side, dh, late=False):
        there = exists(side, dh)
        if (side, dh) in ((-1, 0), (0, -1)):
            there = in_turn(there, origin(side, dh), late)
        pl.when(there)(lambda: copy_of(x, 0, side, dh).start())

    def arrived(x, slot, there=None):
        @pl.when(exists(*SLOTS[slot]) if there is None else there)
        def _():
            pltpu.make_async_copy(
                tiles.at[x, :, slot], tiles.at[x, :, slot], recv_sem.at[x, slot]
            ).wait()

    def pass_on(x, slot, side, there):
        pl.when(there)(lambda: copy_of(x, slot, side, 0).start())

    def forward_upper(x, now=True):
        arrived(x, 4, in_turn(exists(0, 1), at_origin, False) & now)
        pass_on(x, 4, -1, in_turn(exists(-1, 1), origin(-1, 0), False) & now)
        pass_on(x, 4, 1, in_turn(exists(1, 1), origin(0, 0), False) & now)

    def forward_lower(x, late=False, now=True):
        arrived(x, 3, in_turn(exists(0, -1), origin(0, -1), late) & now)
        for side in (-1, 1):
            pass_on(x, 3, side, in_turn(exists(side, -1), origin(0, -1), late) & now)

    def one(there):
        return there.astype(jnp.int32)

    sides = one(along[-1]) + one(along[1])
    expected = sides + one(up_down[-1]) * (1 + sides) - one(near_origin) + 2 * one(at_origin)

    @pl.when(expected > 0)
    def _():
        pl.semaphore_wait(barrier, expected)

    for number, offset in enumerate(AHEAD):
        there = exists(*opposite(offset))
        if opposite(offset) in by_origin:
            there = there & jnp.logical_not(by_origin[opposite(offset)])
        signal(ready.at[number], opposite(offset), there)
    for offset in ((1, 0), (0, 1), (1, 1)):
        signal(ready.at[len(AHEAD)], offset, at_origin)

    def await_ready(number, there):
        pl.when(there)(lambda: pl.semaphore_wait(ready.at[number], 1))

    def await_ahead(number):
        await_ready(number, exists(*AHEAD[number]) & jnp.logical_not(at_origin))

    def send_first(x):
        send(x, 0, -1)
        send(x, -1, 0)
        send(x, 1, 0)
        pl.when(direct)(lambda: direct_copy(x).start())
        pl.when(at_origin)(lambda: copy_of(x, 0, 0, 1).start())

    send_first(K)

    mask_copy.wait()
    for slot, (side, dh) in enumerate(SLOTS):
        if slot == 0:
            bias[slot] = jnp.float32(0)
        else:
            chosen = mask[0, 0, 0, 9 * (side + 1) + 3 * (dh + 1) + 1] != 0
            bias[slot] = jnp.where(exists(side, dh) & chosen, jnp.float32(0), jnp.float32(-FAR))

    for slot in range(1, 9):

        @pl.when(jnp.logical_not(exists(*SLOTS[slot])))
        def _():
            stat_in[slot, :heads] = jnp.full((heads, rows), FAR, F32)
            stat_in[slot, heads:] = jnp.zeros((heads, rows), F32)

            def clear(x, carry):
                tiles[x, :, slot] = jnp.zeros((heads, rows, depth), BF16)
                return carry

            lax.fori_loop(0, 4, clear, 0)

    for copy in locals_:
        copy.wait()

    for head in range(heads):
        product = tiles[G, head, 0].astype(F32) * out_tile[head].astype(F32)
        delta_col[head] = jnp.sum(product, axis=1, keepdims=True)

    def as_row(column):
        return jnp.broadcast_to(column, (rows, 128)).T[:1]

    def score_side(slot, count, index):
        keys = count * rows
        if count == 2:
            lane = lax.broadcasted_iota(jnp.int32, (1, keys), 1)
            bias_row = jnp.where(lane < rows, bias[slot], bias[slot + 1])
        else:
            bias_row = bias[slot]
        for head in range(heads):
            key_rows = tiles[K, head, pl.ds(slot, count)].reshape(keys, depth)
            scores = nt(tiles[Q, head, 0], key_rows) * score_scale + bias_row
            held_scores[index, head, :, :keys] = scores
            top = jnp.max(scores, axis=1, keepdims=True)
            if count == 2:
                old_max = run_max[head]
                top = jnp.maximum(old_max, top)
            total = jnp.sum(jnp.exp2(scores - top), axis=1, keepdims=True)
            if count == 2:
                total = run_sum[head] * jnp.exp2(old_max - top) + total
            run_max[head] = top
            run_sum[head] = total

    def query_side(slot, count, index):
        keys = count * rows
        for head in range(heads):
            key_rows = tiles[K, head, pl.ds(slot, count)].reshape(keys, depth)
            value_rows = tiles[V, head, pl.ds(slot, count)].reshape(keys, depth)
            probs = jnp.exp2(held_scores[index, head, :, :keys] - run_max[head])
            prob_grads = nt(tiles[G, head, 0], value_rows)
            score_grads = (probs * (prob_grads - delta_col[head])).astype(BF16)
            grads = nn(score_grads, key_rows)
            if count == 2:
                dq_acc[head] += grads
            else:
                dq_acc[head] = grads

    def key_side(slot, count, stats):
        queries = count * rows
        for head in range(heads):
            query_rows = tiles[Q, head, pl.ds(slot, count)].reshape(queries, depth)
            grad_rows = tiles[G, head, pl.ds(slot, count)].reshape(queries, depth)
            log_row = [stats[slot + i, head : head + 1] for i in range(count)]
            delta_row = [stats[slot + i, heads + head : heads + head + 1] for i in range(count)]
            if count == 2:
                log_row, delta_row = jnp.concatenate(log_row, 1), jnp.concatenate(delta_row, 1)
            else:
                log_row, delta_row = log_row[0], delta_row[0]
            probs = jnp.exp2(nt(tiles[K, head, 0], query_rows) * score_scale - log_row)
            prob_grads = nt(tiles[V, head, 0], grad_rows)
            score_grads = (probs * (prob_grads - delta_row)).astype(BF16)
            value_part = nn(probs.astype(BF16), grad_rows)
            key_part = nn(score_grads, query_rows)
            if count == 1:
                dv_acc[head] = value_part
                dk_acc[head] = key_part
            else:
                dv_acc[head] += value_part
                dk_acc[head] += key_part

    def arrived_pair(x, slot):
        arrived(x, slot)
        arrived(x, slot + 1)

    shift = one(origin(-1, 0)) + 2 * one(origin(0, -1)) + 2 * one(at_origin)

    def is_empty(step):
        upper = (step == 2) & jnp.logical_not(up_down[1])
        return upper | ((step == 3) & jnp.logical_not(up_down[-1]))

    def step_of(x, side, number):
        step = lax.rem(number + shift, 4)
        for at, slot in ((0, 1), (2, 5), (3, 7)):
            pl.when(step == at)(lambda: arrived_pair(x, slot))
        pl.when(jnp.logical_not(is_empty(step)))(lambda: side(1 + 2 * step, 2, 1 + step))

    def score_step(number):
        step_of(K, score_side, number)

    def query_step(number):
        step_of(V, query_side, number)

    score_side(0, 1, 0)
    send_first(V)
    await_ahead(0)
    for x in (K, V):
        pl.when(exists(0, 1) & jnp.logical_not(at_origin))(lambda: copy_of(x, 0, 0, 1).start())

    def send_all(x):
        for offset in ((0, 1), (1, 0)):
            there = exists(*offset)
            if x == G:
                there = in_turn(there, at_origin, False)
            pl.when(there)(lambda: copy_of(x, 0, *offset).start())
        send(x, 0, -1)
        send(x, -1, 0)
        pl.when(direct)(lambda: direct_copy(x).start())

    send_all(Q)

    @pl.when(at_origin)
    def _():
        copy_of(G, 0, 0, 1).start()
        copy_of(G, 0, 1, 0).start()

    forward_upper(K)
    forward_lower(K)
    score_step(0)
    score_step(1)
    forward_upper(V)
    forward_lower(V)
    send_all(G)
    score_step(2)
    for x in (Q, G):
        forward_upper(x, near_origin)
        forward_lower(x, now=near_origin)

    await_ready(len(AHEAD), by_origin[(-1, 0)] | by_origin[(0, -1)])

    def send_late(x):
        send(x, -1, 0, late=True)
        send(x, 0, -1, late=True)
        pass_on(x, 4, -1, in_turn(exists(-1, 1), origin(-1, 0), True))

    send_late(K)
    forward_lower(K, late=True)
    arrived(K, 4, at_origin)
    send_late(V)
    score_step(3)

    for head in range(heads):
        run_max[head] += jnp.log2(run_sum[head])
    for head in range(heads):
        log_total = as_row(run_max[head])
        delta = as_row(delta_col[head])
        for slot in range(9):
            stat_out[slot, head : head + 1] = log_total - bias[slot]
            stat_out[slot, heads + head : heads + head + 1] = delta

    def stat_copy(slot):
        lands = SLOT_OF[opposite(SLOTS[slot])]
        return pltpu.make_async_remote_copy(
            src_ref=stat_out.at[slot],
            dst_ref=stat_in.at[lands],
            send_sem=stat_send.at[slot],
            recv_sem=stat_recv.at[lands],
            device_id=device(*SLOTS[slot]),
            device_id_type=MESH,
        )

    await_ahead(1)
    await_ahead(2)
    await_ready(len(AHEAD), by_origin[(-1, -1)])
    for slot in range(1, 9):
        if_there(*SLOTS[slot])(lambda: stat_copy(slot).start())

    forward_lower(V, late=True)
    arrived(V, 4, at_origin)
    forward_upper(Q, jnp.logical_not(near_origin))
    forward_lower(Q, now=jnp.logical_not(near_origin))
    query_side(0, 1, 0)
    query_step(0)
    forward_upper(G, jnp.logical_not(near_origin))
    forward_lower(G, now=jnp.logical_not(near_origin))
    send_late(Q)
    send_late(G)
    query_step(1)
    query_step(2)
    query_step(3)
    for x in (Q, G):
        forward_lower(x, late=True)
        arrived(x, 4, at_origin)

    for head in range(heads):
        results[0, head] = (dq_acc[head] * scale).astype(BF16)
    out_copies = [
        pltpu.make_async_copy(results.at[i], out, out_sem.at[i])
        for i, out in enumerate((dq_ref, dk_ref, dv_ref))
    ]
    out_copies[0].start()

    key_side(0, 1, stat_out)

    def stat_arrived(slot):
        @if_there(*SLOTS[slot])
        def _():
            pltpu.make_async_copy(stat_in.at[slot], stat_in.at[slot], stat_recv.at[slot]).wait()

    key_shift = shift + one(origin(-2, -1)) + 2 * one(origin(-1, -2))

    def key_step(number, carry):
        step = lax.rem(number + key_shift, 4)
        for at, slot in enumerate((1, 3, 5, 7)):

            @pl.when(step == at)
            def _():
                stat_arrived(slot)
                stat_arrived(slot + 1)
                if slot != 3:
                    arrived_pair(Q, slot)
                    arrived_pair(G, slot)

        pl.when(jnp.logical_not(is_empty(step)))(lambda: key_side(1 + 2 * step, 2, stat_in))
        return carry

    lax.fori_loop(0, 4, key_step, 0)

    for head in range(heads):
        results[1, head] = (dk_acc[head] * scale).astype(BF16)
    out_copies[1].start()
    for head in range(heads):
        results[2, head] = dv_acc[head].astype(BF16)
    out_copies[2].start()

    for slot in range(1, 9):
        if_there(*SLOTS[slot])(lambda: stat_copy(slot).wait_send())
    for x in (K, V, Q, G):
        for offset in ((0, -1), (0, 1), (-1, 0), (1, 0)):
            if_there(*offset)(lambda: copy_of(x, 0, *offset).wait_send())
        for side in (-1, 1):
            if_there(side, -1)(lambda: copy_of(x, 3, side, 0).wait_send())
        if_there(-1, 1)(lambda: copy_of(x, 4, -1, 0).wait_send())
        pl.when(in_turn(exists(1, 1), origin(0, 0), False))(
            lambda: copy_of(x, 4, 1, 0).wait_send()
        )
        pl.when(direct)(lambda: direct_copy(x).wait_send())
    for copy in out_copies:
        copy.wait()


def settle(*refs):
    sources, targets, (semaphore, held) = refs[:3], refs[3:6], refs[6:]
    loads = [pltpu.make_async_copy(sources[i], held.at[i], semaphore.at[i]) for i in range(3)]
    stores = [pltpu.make_async_copy(held.at[i], targets[i], semaphore.at[3 + i]) for i in range(3)]
    for load in loads:
        load.start()
    for load, store in zip(loads, stores):
        load.wait()
        store.start()
    for store in stores:
        store.wait()


def body(sizes, queries, keys, values, grad_out, attn_out, window_mask):
    shape = queries.shape
    tile = (shape[2],) + shape[4:]
    heads, rows, depth = tile
    flat = [x.reshape(tile) for x in (queries, keys, values, grad_out, attn_out)]
    in_place = pl.BlockSpec(memory_space=pl.ANY)
    outs = pl.pallas_call(
        functools.partial(kernel, sizes),
        out_shape=[jax.ShapeDtypeStruct(tile, BF16)] * 3,
        in_specs=[in_place] * 6,
        out_specs=[in_place] * 3,
        scratch_shapes=[
            pltpu.SMEM(window_mask.shape, jnp.int32),
            pltpu.VMEM((3,) + tile, BF16),
            pltpu.VMEM((4, heads, 9, rows, depth), BF16),
            pltpu.VMEM(tile, BF16),
            pltpu.VMEM((9, 2 * heads, rows), F32),
            pltpu.VMEM((9, 2 * heads, rows), F32),
            pltpu.SMEM((9,), F32),
            pltpu.VMEM((5, heads, rows, 2 * rows), F32),
            pltpu.VMEM((heads, rows, 1), F32),
            pltpu.VMEM((heads, rows, 1), F32),
            pltpu.VMEM((heads, rows, 1), F32),
            pltpu.VMEM(tile, F32),
            pltpu.VMEM(tile, F32),
            pltpu.VMEM(tile, F32),
            pltpu.SemaphoreType.DMA((5,)),
            pltpu.SemaphoreType.DMA((4, 9)),
            pltpu.SemaphoreType.DMA((4, 9)),
            pltpu.SemaphoreType.DMA((9,)),
            pltpu.SemaphoreType.DMA((9,)),
            pltpu.SemaphoreType.REGULAR((len(AHEAD) + 1,)),
            pltpu.SemaphoreType.DMA,
            pltpu.SemaphoreType.DMA((3,)),
        ],
        compiler_params=pltpu.CompilerParams(
            collective_id=0, has_side_effects=True, vmem_limit_bytes=54 << 20
        ),
        name="tile_attention_backward",
    )(window_mask, *flat)
    outs = pl.pallas_call(
        settle,
        out_shape=[jax.ShapeDtypeStruct(tile, BF16)] * 3,
        in_specs=[in_place] * 3,
        out_specs=[in_place] * 3,
        scratch_shapes=[pltpu.SemaphoreType.DMA((6,)), pltpu.VMEM((3,) + tile, BF16)],
        compiler_params=pltpu.CompilerParams(vmem_limit_bytes=54 << 20),
        name="settle",
    )(*outs)
    return tuple(x.reshape(shape) for x in outs)


def solution(mesh):
    sizes = (mesh.shape["tm"], mesh.shape["height"])
    tiled = P("tm", "height", "dp", None, None, None)
    return jax.shard_map(
        functools.partial(body, sizes),
        mesh=mesh,
        in_specs=(tiled,) * 5 + (P("tm", "height", None, None),),
        out_specs=(tiled,) * 3,
        check_vma=False,
    )
```

```python
import functools

import jax
import jax.numpy as jnp
from jax import lax
from jax.experimental import pallas as pl
from jax.experimental.pallas import tpu as pltpu
from jax.sharding import PartitionSpec as P

MESH = pl.DeviceIdType.MESH
F32 = jnp.float32
BF16 = jnp.bfloat16
LOG2E = 1.4426950408889634
FAR = 1e30

SLOTS = ((0, 0), (-1, 0), (1, 0), (0, -1), (0, 1), (-1, 1), (1, 1), (-1, -1), (1, -1))
AHEAD = ((0, 1), (-1, 1), (1, 1))
SLOT_OF = {offset: slot for slot, offset in enumerate(SLOTS)}
K, V, Q, G = range(4)


def nt(a, b):
    return lax.dot_general(a, b, (((1,), (1,)), ((), ())), preferred_element_type=F32)


def nn(a, b):
    return lax.dot_general(a, b, (((1,), (0,)), ((), ())), preferred_element_type=F32)


def kernel(
    sizes,
    mask_ref,
    q_ref,
    k_ref,
    v_ref,
    g_ref,
    o_ref,
    dq_ref,
    dk_ref,
    dv_ref,
    mask,
    results,
    tiles,
    out_tile,
    stat_out,
    stat_in,
    bias,
    held_scores,
    run_max,
    run_sum,
    delta_col,
    dq_acc,
    dk_acc,
    dv_acc,
    local_sem,
    send_sem,
    recv_sem,
    stat_send,
    stat_recv,
    ready,
    mask_sem,
    out_sem,
):
    n_t, n_h = sizes
    heads, rows, depth = q_ref.shape
    scale = depth**-0.5
    score_scale = scale * LOG2E
    t = lax.axis_index("tm")
    h = lax.axis_index("height")
    d = lax.axis_index("dp")
    along = {-1: t > 0, 1: t < n_t - 1}
    up_down = {-1: h > 0, 1: h < n_h - 1}

    def exists(side, dh):
        if side == 0:
            return up_down[dh]
        return along[side] if dh == 0 else along[side] & up_down[dh]

    def origin(side, dh):
        return (t + side == 0) & (h + dh == 0) & (d == 0)

    direct = (t == 0) & (h == 1) & (d == 0)

    def device(side, dh):
        return (t + side, h + dh, d)

    def if_there(side, dh):
        return pl.when(exists(side, dh))

    def opposite(offset):
        return (-offset[0], -offset[1])

    barrier = pltpu.get_barrier_semaphore()
    at_origin = origin(0, 0)
    by_origin = {offset: origin(*offset) for offset in ((-1, 0), (0, -1), (-1, -1))}
    near_origin = by_origin[(-1, 0)] | by_origin[(0, -1)] | by_origin[(-1, -1)]

    def signal(semaphore, offset, there):
        @pl.when(there)
        def _():
            pl.semaphore_signal(semaphore, inc=1, device_id=device(*offset), device_id_type=MESH)

    for offset in AHEAD + ((-1, 0), (1, 0)):
        signal(barrier, offset, exists(*offset) & jnp.logical_not(at_origin))
    for offset in ((0, -1), (-1, -1)):
        signal(barrier, offset, by_origin[offset])

    sources = {K: k_ref, V: v_ref, Q: q_ref, G: g_ref}
    locals_ = [
        pltpu.make_async_copy(sources[x], tiles.at[x, :, 0], local_sem.at[x]) for x in (K, V, Q, G)
    ]
    locals_.append(pltpu.make_async_copy(o_ref, out_tile, local_sem.at[4]))
    mask_copy = pltpu.make_async_copy(mask_ref, mask, mask_sem)
    mask_copy.start()
    for copy in locals_:
        copy.start()

    def copy_of(x, from_slot, side, dh):
        own_side, own_dh = SLOTS[from_slot]
        lands = SLOT_OF[(own_side - side, own_dh - dh)]
        return pltpu.make_async_remote_copy(
            src_ref=sources[x] if from_slot == 0 else tiles.at[x, :, from_slot],
            dst_ref=tiles.at[x, :, lands],
            send_sem=send_sem.at[x, lands],
            recv_sem=recv_sem.at[x, lands],
            device_id=device(side, dh),
            device_id_type=MESH,
        )

    def direct_copy(x):
        slot = SLOT_OF[(-1, 1)]
        return pltpu.make_async_remote_copy(
            src_ref=sources[x],
            dst_ref=tiles.at[x, :, slot],
            send_sem=send_sem.at[x, 0],
            recv_sem=recv_sem.at[x, slot],
            device_id=device(1, -1),
            device_id_type=MESH,
        )

    def in_turn(there, at_origin, late):
        return there & (at_origin if late else jnp.logical_not(at_origin))

    def send(x, side, dh, late=False):
        there = exists(side, dh)
        if (side, dh) in ((-1, 0), (0, -1)):
            there = in_turn(there, origin(side, dh), late)
        pl.when(there)(lambda: copy_of(x, 0, side, dh).start())

    def arrived(x, slot, there=None):
        @pl.when(exists(*SLOTS[slot]) if there is None else there)
        def _():
            pltpu.make_async_copy(
                tiles.at[x, :, slot], tiles.at[x, :, slot], recv_sem.at[x, slot]
            ).wait()

    def pass_on(x, slot, side, there):
        pl.when(there)(lambda: copy_of(x, slot, side, 0).start())

    def forward_upper(x, now=True):
        arrived(x, 4, in_turn(exists(0, 1), at_origin, False) & now)
        pass_on(x, 4, -1, in_turn(exists(-1, 1), origin(-1, 0), False) & now)
        pass_on(x, 4, 1, in_turn(exists(1, 1), origin(0, 0), False) & now)

    def forward_lower(x, late=False, now=True):
        arrived(x, 3, in_turn(exists(0, -1), origin(0, -1), late) & now)
        for side in (-1, 1):
            pass_on(x, 3, side, in_turn(exists(side, -1), origin(0, -1), late) & now)

    def one(there):
        return there.astype(jnp.int32)

    sides = one(along[-1]) + one(along[1])
    expected = sides + one(up_down[-1]) * (1 + sides) - one(near_origin) + 2 * one(at_origin)

    @pl.when(expected > 0)
    def _():
        pl.semaphore_wait(barrier, expected)

    for number, offset in enumerate(AHEAD):
        there = exists(*opposite(offset))
        if opposite(offset) in by_origin:
            there = there & jnp.logical_not(by_origin[opposite(offset)])
        signal(ready.at[number], opposite(offset), there)
    for offset in ((1, 0), (0, 1), (1, 1)):
        signal(ready.at[len(AHEAD)], offset, at_origin)

    def await_ready(number, there):
        pl.when(there)(lambda: pl.semaphore_wait(ready.at[number], 1))

    def await_ahead(number):
        await_ready(number, exists(*AHEAD[number]) & jnp.logical_not(at_origin))

    for x in (K, V):
        send(x, 0, -1)
        send(x, -1, 0)
        send(x, 1, 0)
        pl.when(direct)(lambda: direct_copy(x).start())
        pl.when(at_origin)(lambda: copy_of(x, 0, 0, 1).start())

    mask_copy.wait()
    for slot, (side, dh) in enumerate(SLOTS):
        if slot == 0:
            bias[slot] = jnp.float32(0)
        else:
            chosen = mask[0, 0, 0, 9 * (side + 1) + 3 * (dh + 1) + 1] != 0
            bias[slot] = jnp.where(exists(side, dh) & chosen, jnp.float32(0), jnp.float32(-FAR))

    for slot in range(1, 9):

        @pl.when(jnp.logical_not(exists(*SLOTS[slot])))
        def _():
            stat_in[slot, :heads] = jnp.full((heads, rows), FAR, F32)
            stat_in[slot, heads:] = jnp.zeros((heads, rows), F32)

            def clear(x, carry):
                tiles[x, :, slot] = jnp.zeros((heads, rows, depth), BF16)
                return carry

            lax.fori_loop(0, 4, clear, 0)

    for copy in locals_:
        copy.wait()

    for head in range(heads):
        product = tiles[G, head, 0].astype(F32) * out_tile[head].astype(F32)
        delta_col[head] = jnp.sum(product, axis=1, keepdims=True)

    def as_row(column):
        return jnp.broadcast_to(column, (rows, 128)).T[:1]

    def score_side(slot, count, index):
        keys = count * rows
        if count == 2:
            lane = lax.broadcasted_iota(jnp.int32, (1, keys), 1)
            bias_row = jnp.where(lane < rows, bias[slot], bias[slot + 1])
        else:
            bias_row = bias[slot]
        for head in range(heads):
            key_rows = tiles[K, head, pl.ds(slot, count)].reshape(keys, depth)
            scores = nt(tiles[Q, head, 0], key_rows) * score_scale + bias_row
            held_scores[index, head, :, :keys] = scores
            top = jnp.max(scores, axis=1, keepdims=True)
            if count == 2:
                old_max = run_max[head]
                top = jnp.maximum(old_max, top)
            total = jnp.sum(jnp.exp2(scores - top), axis=1, keepdims=True)
            if count == 2:
                total = run_sum[head] * jnp.exp2(old_max - top) + total
            run_max[head] = top
            run_sum[head] = total

    def query_side(slot, count, index):
        keys = count * rows
        for head in range(heads):
            key_rows = tiles[K, head, pl.ds(slot, count)].reshape(keys, depth)
            value_rows = tiles[V, head, pl.ds(slot, count)].reshape(keys, depth)
            probs = jnp.exp2(held_scores[index, head, :, :keys] - run_max[head])
            prob_grads = nt(tiles[G, head, 0], value_rows)
            score_grads = (probs * (prob_grads - delta_col[head])).astype(BF16)
            grads = nn(score_grads, key_rows)
            if count == 2:
                dq_acc[head] += grads
            else:
                dq_acc[head] = grads

    def key_side(slot, count, stats):
        queries = count * rows
        for head in range(heads):
            query_rows = tiles[Q, head, pl.ds(slot, count)].reshape(queries, depth)
            grad_rows = tiles[G, head, pl.ds(slot, count)].reshape(queries, depth)
            log_row = [stats[slot + i, head : head + 1] for i in range(count)]
            delta_row = [stats[slot + i, heads + head : heads + head + 1] for i in range(count)]
            if count == 2:
                log_row, delta_row = jnp.concatenate(log_row, 1), jnp.concatenate(delta_row, 1)
            else:
                log_row, delta_row = log_row[0], delta_row[0]
            probs = jnp.exp2(nt(tiles[K, head, 0], query_rows) * score_scale - log_row)
            prob_grads = nt(tiles[V, head, 0], grad_rows)
            score_grads = (probs * (prob_grads - delta_row)).astype(BF16)
            value_part = nn(probs.astype(BF16), grad_rows)
            key_part = nn(score_grads, query_rows)
            if count == 1:
                dv_acc[head] = value_part
                dk_acc[head] = key_part
            else:
                dv_acc[head] += value_part
                dk_acc[head] += key_part

    def arrived_pair(x, slot):
        arrived(x, slot)
        arrived(x, slot + 1)

    shift = one(origin(-1, 0)) + 2 * one(origin(0, -1)) + 2 * one(at_origin)

    def is_empty(step):
        upper = (step == 2) & jnp.logical_not(up_down[1])
        return upper | ((step == 3) & jnp.logical_not(up_down[-1]))

    def step_of(x, side, number):
        step = lax.rem(number + shift, 4)
        for at, slot in ((0, 1), (2, 5), (3, 7)):
            pl.when(step == at)(lambda: arrived_pair(x, slot))
        pl.when(jnp.logical_not(is_empty(step)))(lambda: side(1 + 2 * step, 2, 1 + step))

    def score_step(number):
        step_of(K, score_side, number)

    def query_step(number):
        step_of(V, query_side, number)

    score_side(0, 1, 0)
    await_ahead(0)
    for x in (K, V):
        pl.when(exists(0, 1) & jnp.logical_not(at_origin))(lambda: copy_of(x, 0, 0, 1).start())

    def send_all(x):
        for offset in ((0, 1), (1, 0)):
            there = exists(*offset)
            if x == G:
                there = in_turn(there, at_origin, False)
            pl.when(there)(lambda: copy_of(x, 0, *offset).start())
        send(x, 0, -1)
        send(x, -1, 0)
        pl.when(direct)(lambda: direct_copy(x).start())

    send_all(Q)

    @pl.when(at_origin)
    def _():
        copy_of(G, 0, 0, 1).start()
        copy_of(G, 0, 1, 0).start()

    forward_upper(K)
    forward_lower(K)
    score_step(0)
    score_step(1)
    forward_upper(V)
    forward_lower(V)
    send_all(G)
    score_step(2)
    for x in (Q, G):
        forward_upper(x, near_origin)
        forward_lower(x, now=near_origin)

    await_ready(len(AHEAD), by_origin[(-1, 0)] | by_origin[(0, -1)])
    for x in (K, V):
        send(x, -1, 0, late=True)
        send(x, 0, -1, late=True)
        pass_on(x, 4, -1, in_turn(exists(-1, 1), origin(-1, 0), True))
    forward_lower(K, late=True)
    arrived(K, 4, at_origin)
    score_step(3)

    for head in range(heads):
        run_max[head] += jnp.log2(run_sum[head])
    for head in range(heads):
        log_total = as_row(run_max[head])
        delta = as_row(delta_col[head])
        for slot in range(9):
            stat_out[slot, head : head + 1] = log_total - bias[slot]
            stat_out[slot, heads + head : heads + head + 1] = delta

    def stat_copy(slot):
        lands = SLOT_OF[opposite(SLOTS[slot])]
        return pltpu.make_async_remote_copy(
            src_ref=stat_out.at[slot],
            dst_ref=stat_in.at[lands],
            send_sem=stat_send.at[slot],
            recv_sem=stat_recv.at[lands],
            device_id=device(*SLOTS[slot]),
            device_id_type=MESH,
        )

    await_ahead(1)
    await_ahead(2)
    await_ready(len(AHEAD), by_origin[(-1, -1)])
    for slot in range(1, 9):
        if_there(*SLOTS[slot])(lambda: stat_copy(slot).start())

    forward_lower(V, late=True)
    arrived(V, 4, at_origin)
    forward_upper(Q, jnp.logical_not(near_origin))
    forward_lower(Q, now=jnp.logical_not(near_origin))
    query_side(0, 1, 0)
    query_step(0)
    forward_upper(G, jnp.logical_not(near_origin))
    forward_lower(G, now=jnp.logical_not(near_origin))
    for x in (Q, G):
        send(x, -1, 0, late=True)
        send(x, 0, -1, late=True)
        pass_on(x, 4, -1, in_turn(exists(-1, 1), origin(-1, 0), True))
    query_step(1)
    query_step(2)
    query_step(3)
    for x in (Q, G):
        forward_lower(x, late=True)
        arrived(x, 4, at_origin)

    for head in range(heads):
        results[0, head] = (dq_acc[head] * scale).astype(BF16)
    out_copies = [
        pltpu.make_async_copy(results.at[i], out, out_sem.at[i])
        for i, out in enumerate((dq_ref, dk_ref, dv_ref))
    ]
    out_copies[0].start()

    key_side(0, 1, stat_out)

    def stat_arrived(slot):
        @if_there(*SLOTS[slot])
        def _():
            pltpu.make_async_copy(stat_in.at[slot], stat_in.at[slot], stat_recv.at[slot]).wait()

    def key_step(number, carry):
        step = lax.rem(number + shift, 4)
        for at, slot in enumerate((1, 3, 5, 7)):

            @pl.when(step == at)
            def _():
                stat_arrived(slot)
                stat_arrived(slot + 1)
                if slot != 3:
                    arrived_pair(Q, slot)
                    arrived_pair(G, slot)

        pl.when(jnp.logical_not(is_empty(step)))(lambda: key_side(1 + 2 * step, 2, stat_in))
        return carry

    lax.fori_loop(0, 4, key_step, 0)

    for head in range(heads):
        results[1, head] = (dk_acc[head] * scale).astype(BF16)
    out_copies[1].start()
    for head in range(heads):
        results[2, head] = dv_acc[head].astype(BF16)
    out_copies[2].start()

    for slot in range(1, 9):
        if_there(*SLOTS[slot])(lambda: stat_copy(slot).wait_send())
    for x in (K, V, Q, G):
        for offset in ((0, -1), (0, 1), (-1, 0), (1, 0)):
            if_there(*offset)(lambda: copy_of(x, 0, *offset).wait_send())
        for side in (-1, 1):
            if_there(side, -1)(lambda: copy_of(x, 3, side, 0).wait_send())
        if_there(-1, 1)(lambda: copy_of(x, 4, -1, 0).wait_send())
        pl.when(in_turn(exists(1, 1), origin(0, 0), False))(
            lambda: copy_of(x, 4, 1, 0).wait_send()
        )
        pl.when(direct)(lambda: direct_copy(x).wait_send())
    for copy in out_copies:
        copy.wait()


def settle(*refs):
    sources, targets, (semaphore, held) = refs[:3], refs[3:6], refs[6:]
    loads = [pltpu.make_async_copy(sources[i], held.at[i], semaphore.at[i]) for i in range(3)]
    stores = [pltpu.make_async_copy(held.at[i], targets[i], semaphore.at[3 + i]) for i in range(3)]
    for load in loads:
        load.start()
    for load, store in zip(loads, stores):
        load.wait()
        store.start()
    for store in stores:
        store.wait()


def body(sizes, queries, keys, values, grad_out, attn_out, window_mask):
    shape = queries.shape
    tile = (shape[2],) + shape[4:]
    heads, rows, depth = tile
    flat = [x.reshape(tile) for x in (queries, keys, values, grad_out, attn_out)]
    in_place = pl.BlockSpec(memory_space=pl.ANY)
    outs = pl.pallas_call(
        functools.partial(kernel, sizes),
        out_shape=[jax.ShapeDtypeStruct(tile, BF16)] * 3,
        in_specs=[in_place] * 6,
        out_specs=[in_place] * 3,
        scratch_shapes=[
            pltpu.SMEM(window_mask.shape, jnp.int32),
            pltpu.VMEM((3,) + tile, BF16),
            pltpu.VMEM((4, heads, 9, rows, depth), BF16),
            pltpu.VMEM(tile, BF16),
            pltpu.VMEM((9, 2 * heads, rows), F32),
            pltpu.VMEM((9, 2 * heads, rows), F32),
            pltpu.SMEM((9,), F32),
            pltpu.VMEM((5, heads, rows, 2 * rows), F32),
            pltpu.VMEM((heads, rows, 1), F32),
            pltpu.VMEM((heads, rows, 1), F32),
            pltpu.VMEM((heads, rows, 1), F32),
            pltpu.VMEM(tile, F32),
            pltpu.VMEM(tile, F32),
            pltpu.VMEM(tile, F32),
            pltpu.SemaphoreType.DMA((5,)),
            pltpu.SemaphoreType.DMA((4, 9)),
            pltpu.SemaphoreType.DMA((4, 9)),
            pltpu.SemaphoreType.DMA((9,)),
            pltpu.SemaphoreType.DMA((9,)),
            pltpu.SemaphoreType.REGULAR((len(AHEAD) + 1,)),
            pltpu.SemaphoreType.DMA,
            pltpu.SemaphoreType.DMA((3,)),
        ],
        compiler_params=pltpu.CompilerParams(
            collective_id=0, has_side_effects=True, vmem_limit_bytes=54 << 20
        ),
        name="tile_attention_backward",
    )(window_mask, *flat)
    outs = pl.pallas_call(
        settle,
        out_shape=[jax.ShapeDtypeStruct(tile, BF16)] * 3,
        in_specs=[in_place] * 3,
        out_specs=[in_place] * 3,
        scratch_shapes=[pltpu.SemaphoreType.DMA((6,)), pltpu.VMEM((3,) + tile, BF16)],
        compiler_params=pltpu.CompilerParams(vmem_limit_bytes=54 << 20),
        name="settle",
    )(*outs)
    return tuple(x.reshape(shape) for x in outs)


def solution(mesh):
    sizes = (mesh.shape["tm"], mesh.shape["height"])
    tiled = P("tm", "height", "dp", None, None, None)
    return jax.shard_map(
        functools.partial(body, sizes),
        mesh=mesh,
        in_specs=(tiled,) * 5 + (P("tm", "height", None, None),),
        out_specs=(tiled,) * 3,
        check_vma=False,
    )
```
